512 devices in a mesh: tm: 16 (over y, core), chan: 32 (over z, x).
Axes of the slice: x: 4, y: 8, z: 8, core: 2. Of those that a mesh axis runs over, the one named last changes fastest.
Arguments:
- strain: float32 [1024, 65536], P('chan', 'tm'), may hold values from -16 to 16
- channel_mask: int32 [1024], P('chan'), may hold values 0 or 1
Outputs:
- cleaned: float32 [1024, 65536], P('chan', 'tm')
The draws below stay inside these ranges and needn't reach their ends.
All inputs are finite; a program needn't handle non-finite values. No bound on the sum of `channel_mask` on one device may be relied on, other than what follows from the above.
Results may differ from the reference program's by a relative error of at most 0.0003.
Values sent between devices are 32-bit elements; how exact they have to be, the bound alone decides.
A program may use at most 64 MiB of HBM per device.

```python
import math
import jax
import jax.numpy as jnp
import numpy as np
from jax import lax

RADIUS = 16
NCH = 1024
READING_COUNT = 65536


def draw_strain(key, part):
    subkeys = jax.random.split(key, 9)
    clock_readings = jnp.arange(READING_COUNT, dtype=jnp.float32)
    sinusoid_hertz = jnp.exp(jax.random.uniform(subkeys[0], (NCH, 1), jnp.float32, math.log(2e-05), math.log(0.0001)))
    sinusoid_angles = jax.random.uniform(subkeys[1], (NCH, 1), jnp.float32, -math.pi, math.pi)
    tone_steps = jax.random.randint(subkeys[6], (NCH, 1), 737, 1025).astype(jnp.int32)
    tone_clock = jnp.arange(READING_COUNT, dtype=jnp.int32)[None, :]
    tone_turns = (tone_clock * tone_steps % 4096).astype(jnp.float32) / 4096.0
    tone_angles = jax.random.uniform(subkeys[7], (NCH, 1), jnp.float32, -math.pi, math.pi)
    tone_wave = jnp.sin(2.0 * math.pi * tone_turns + tone_angles)
    gaussian_jitter = 0.5 * jnp.clip(jax.random.normal(subkeys[3], (NCH, READING_COUNT), jnp.float32), -6.0, 6.0)
    sensor_shifts = jax.random.uniform(subkeys[4], (NCH, 1), jnp.float32, -3.0, 3.0)
    oscillation_height = jax.random.uniform(subkeys[5], (NCH, 1), jnp.float32, 0.5, 2.0)
    tone_height = jax.random.uniform(subkeys[8], (NCH, 1), jnp.float32, 6.0, 8.0)
    slow_wave = oscillation_height * jnp.sin(2.0 * math.pi * sinusoid_hertz * clock_readings[None, :] + sinusoid_angles)
    return gaussian_jitter + sensor_shifts + slow_wave + tone_height * tone_wave


def set_ends(result, stream_key, low, top_value):
    dims = result.shape
    place = [jax.random.randint(jax.random.fold_in(stream_key, axis), (), 0, dims[axis]) for axis in range(len(dims))]
    result = result.at[tuple(place)].set(low)
    longest = dims.index(max(dims))
    place[longest] = (place[longest] + 1) % dims[longest]
    return result.at[tuple(place)].set(top_value)


def setup_inputs(seed: int = 0) -> dict:
    seeds = jax.random.split(jax.random.key(seed), 3)
    return {
        "strain": draw_strain(jax.random.fold_in(seeds[2], 71), 0),
        "channel_mask": set_ends((jax.random.randint(seeds[1], (NCH,), 0, 8) < 7).astype(jnp.int32), jax.random.fold_in(seeds[1], 1), 0, 1),
    }


low_corner = 0.015
high_corner = 100.0
sample_rate = 500.0
highest = lax.Precision.HIGHEST

def section(corner, highpass):
    warped = 2.0 * sample_rate * math.tan(math.pi * corner / sample_rate)
    scaled = warped / (2.0 * sample_rate * math.sqrt(2.0))
    numer_real = 1.0 - scaled
    numer_imag = scaled
    denom_real = 1.0 + scaled
    denom_imag = -scaled
    modulus = denom_real * denom_real + denom_imag * denom_imag
    pole_real = (numer_real * denom_real + numer_imag * denom_imag) / modulus
    pole_imag = (numer_imag * denom_real - numer_real * denom_imag) / modulus
    pole_norm = pole_real * pole_real + pole_imag * pole_imag
    zero_place = 1.0 if highpass else -1.0
    section_gain = ((1.0 + zero_place * pole_real) ** 2 + pole_imag * pole_imag) / 4.0
    linear = section_gain * (2.0 * pole_real - 2.0 * zero_place)
    constant = section_gain * (1.0 - pole_norm)
    shrink = 1.0 - math.sqrt(pole_norm)
    first_out = linear / shrink
    second = (constant + pole_real * linear) / (pole_imag * shrink)
    rotation = np.array([[pole_real, -pole_imag], [pole_imag, pole_real]])
    inject = np.array([shrink, 0.0])
    return (rotation, inject, np.array([first_out, second]), section_gain)

def filter_system():
    high_rotation, high_inject, high_out, high_gain = section(low_corner, True)
    low_rotation, low_inject, low_out, low_gain = section(high_corner, False)
    upper_rows = np.concatenate([high_rotation, np.zeros((2, 2))], axis=1)
    lower_rows = np.concatenate([np.outer(low_inject, high_out), low_rotation], axis=1)
    transition = np.concatenate([upper_rows, lower_rows], axis=0)
    driving = np.concatenate([high_inject, low_inject * high_gain])
    readout = np.concatenate([high_out * low_gain, low_out])
    direct = low_gain * high_gain
    return (transition, driving, readout, direct)

def spatial_taps(extent):
    positions = np.arange(-extent, extent + 1)
    window = 0.5 * (1.0 + np.cos(np.pi * positions / (extent + 1)))
    window = window / np.sum(window)
    return np.where(positions == 0, 1.0 - window, -window)

def run_filter(record):
    transition, driving, readout, direct = filter_system()
    transition = jnp.asarray(transition, jnp.float32)
    driving = jnp.asarray(driving, jnp.float32)
    readout = jnp.asarray(readout, jnp.float32)
    direct = jnp.asarray(direct, jnp.float32)

    def advance(current, column):
        output = jnp.dot(readout, current, precision=highest) + direct * column
        current = jnp.dot(transition, current, precision=highest) + driving[:, None] * column[None, :]
        return (current, output)
    initial = jnp.zeros((4, record.shape[0]), jnp.float32)
    unused, outputs = lax.scan(advance, initial, record.T)
    return outputs.T

def reference(strain, channel_mask):
    forward = run_filter(strain)
    backward = run_filter(forward[:, ::-1])[:, ::-1]
    masked = backward * channel_mask.astype(jnp.float32)[:, None]
    taps = spatial_taps(RADIUS)
    padded = jnp.pad(masked, ((RADIUS, RADIUS), (0, 0)))
    cleaned = jnp.zeros_like(masked)
    for offset_step in range(2 * RADIUS + 1):
        cleaned = cleaned + jnp.float32(taps[offset_step]) * padded[offset_step:offset_step + NCH]
    return cleaned
```

```python
import functools
import math

import jax
import jax.numpy as jnp
import ml_dtypes
import numpy as np
from jax import lax
from jax.experimental import pallas as pl
from jax.experimental.pallas import tpu as pltpu
from jax.sharding import PartitionSpec as P

RADIUS = 16
BLOCK = 256
LANES = 128
PIECES = 4

low_corner = 0.015
high_corner = 100.0
sample_rate = 500.0
highest = lax.Precision.HIGHEST
MESH = pl.DeviceIdType.MESH


def section(corner, highpass):
    warped = 2.0 * sample_rate * math.tan(math.pi * corner / sample_rate)
    scaled = warped / (2.0 * sample_rate * math.sqrt(2.0))
    numer_real = 1.0 - scaled
    denom_real = 1.0 + scaled
    denom_imag = -scaled
    modulus = denom_real * denom_real + denom_imag * denom_imag
    pole_real = (numer_real * denom_real + scaled * denom_imag) / modulus
    pole_imag = (scaled * denom_real - numer_real * denom_imag) / modulus
    pole_norm = pole_real * pole_real + pole_imag * pole_imag
    zero_place = 1.0 if highpass else -1.0
    section_gain = ((1.0 + zero_place * pole_real) ** 2 + pole_imag * pole_imag) / 4.0
    linear = section_gain * (2.0 * pole_real - 2.0 * zero_place)
    constant = section_gain * (1.0 - pole_norm)
    shrink = 1.0 - math.sqrt(pole_norm)
    first_out = linear / shrink
    second = (constant + pole_real * linear) / (pole_imag * shrink)
    rotation = np.array([[pole_real, -pole_imag], [pole_imag, pole_real]])
    inject = np.array([shrink, 0.0])
    return (rotation, inject, np.array([first_out, second]), section_gain)


def filter_system():
    high_rotation, high_inject, high_out, high_gain = section(low_corner, True)
    low_rotation, low_inject, low_out, low_gain = section(high_corner, False)
    upper_rows = np.concatenate([high_rotation, np.zeros((2, 2))], axis=1)
    lower_rows = np.concatenate([np.outer(low_inject, high_out), low_rotation], axis=1)
    transition = np.concatenate([upper_rows, lower_rows], axis=0)
    driving = np.concatenate([high_inject, low_inject * high_gain])
    readout = np.concatenate([high_out * low_gain, low_out])
    direct = low_gain * high_gain
    return (transition, driving, readout, direct)


def spatial_taps(extent):
    positions = np.arange(-extent, extent + 1)
    window = 0.5 * (1.0 + np.cos(np.pi * positions / (extent + 1)))
    window = window / np.sum(window)
    return np.where(positions == 0, 1.0 - window, -window)


def chain(count, power, couple):
    powers = [np.eye(4)]
    for _ in range(count):
        powers.append(powers[-1] @ power)
    ahead = np.zeros((count, 4, count, 8))
    behind = np.zeros((count, 4, count, 8))
    for at in range(count):
        for other in range(at):
            ahead[at, :, other, :4] = powers[at - 1 - other]
    for at in range(count):
        for other in range(at + 1, count):
            gives = np.einsum("pq,qjr->pjr", couple, ahead[other])
            gives[:, other, 4:] += np.eye(4)
            behind[at] += np.einsum("pq,qjr->pjr", powers[other - 1 - at], gives)
    inner = np.concatenate([ahead, behind], axis=1)
    outer = np.zeros((count, 8, 8))
    for at in range(count):
        outer[at, :4, :4] = powers[at]
    for at in range(count):
        outer[at, 4:, 4:] = powers[count - 1 - at]
        for other in range(at + 1, count):
            outer[at, 4:, :4] += powers[other - 1 - at] @ couple @ outer[other, :4, :4]
    total = np.zeros((8, count, 8))
    for other in range(count):
        total[:4, other, :4] = powers[count - 1 - other]
        gives = np.einsum("pq,qjr->pjr", couple, ahead[other])
        gives[:, other, 4:] += np.eye(4)
        total[4:] += np.einsum("pq,qjr->pjr", powers[other], gives)
    pull = sum(powers[other] @ couple @ powers[other] for other in range(count))
    return inner, outer, total, powers[count], pull


def split(table):
    high = np.asarray(table, np.float32).astype(ml_dtypes.bfloat16)
    low = (np.asarray(table, np.float64) - high.astype(np.float64)).astype(np.float32)
    return high, low.astype(ml_dtypes.bfloat16)


def thrice(table):
    high, low = split(table)
    return np.concatenate([high, high, low], axis=0)


@functools.lru_cache(maxsize=None)
def filter_tables(blocks, devices):
    transition, driving, readout, direct = filter_system()
    powers = [np.eye(4)]
    for _ in range(BLOCK):
        powers.append(powers[-1] @ transition)
    response = np.array([direct] + [readout @ powers[lag] @ driving for lag in range(BLOCK - 1)])
    lag = np.arange(BLOCK)[:, None] - np.arange(BLOCK)[None, :]
    forward = np.where(lag >= 0, response[np.clip(lag, 0, BLOCK - 1)], 0.0)
    observe = np.stack([readout @ powers[at] for at in range(BLOCK)])
    reach = np.stack([powers[BLOCK - 1 - at] @ driving for at in range(BLOCK)], axis=1)
    both_ways = forward.T @ forward
    gives = np.concatenate([reach, reach[:, ::-1] @ forward], axis=0)
    takes = np.concatenate([forward.T @ observe, observe[::-1]], axis=1)
    couple = reach[:, ::-1] @ observe
    inner, outer, total, power, pull = chain(blocks, powers[BLOCK], couple)
    across = chain(devices, power, pull)[0]
    width = 8 * blocks
    first = thrice(np.tile(gives.T, (1, blocks)))
    main = thrice(np.concatenate([np.tile(gives.T, (1, blocks)), both_ways], axis=1))
    correct = thrice(np.tile(takes.T, (blocks, 1)))
    return (
        first,
        main,
        correct,
        np.asarray(inner.reshape(width, width).T, np.float32),
        np.asarray(total.reshape(8, width), np.float32),
        np.asarray(outer.reshape(width, 8).T, np.float32),
        np.asarray(across.reshape(devices, 8, devices * 8), np.float32),
    )


@functools.lru_cache(maxsize=None)
def space_tables(channels):
    taps = spatial_taps(RADIUS)

    def band(sources):
        lag = np.asarray(sources)[None, :] - np.arange(channels)[:, None] + RADIUS
        inside = (lag >= 0) & (lag <= 2 * RADIUS)
        return np.where(inside, taps[np.clip(lag, 0, 2 * RADIUS)], 0.0)

    own = band(np.arange(channels))
    edge = np.concatenate(
        [band(np.arange(-RADIUS, 0)), band(np.arange(channels, channels + RADIUS))], axis=1
    )
    parts = []
    for table in (edge, own):
        high, low = split(table)
        parts += [high, low, high]
    states = np.zeros((channels, 3 * LANES))
    states[:, :channels] = own
    states[:, LANES : LANES + channels] = band(np.arange(-channels, 0))
    states[:, 2 * LANES : 2 * LANES + channels] = band(np.arange(channels, 2 * channels))
    return np.concatenate(parts, axis=1), np.asarray(states, np.float32)


def halves(value):
    high = value.astype(jnp.bfloat16)
    return high, (value - high.astype(jnp.float32)).astype(jnp.bfloat16)


def kernel(
    devices,
    groups,
    x_hbm,
    mask_hbm,
    first_hbm,
    main_hbm,
    correct_hbm,
    inner_hbm,
    total_hbm,
    outer_hbm,
    across_hbm,
    space_hbm,
    states_hbm,
    out_hbm,
    x,
    mask,
    first,
    main,
    correct,
    inner,
    total,
    outer,
    across,
    space,
    states,
    halo,
    ends,
    entering,
    plain,
    result,
    load_sem,
    end_send,
    end_recv,
    near_send,
    near_recv,
    halo_send,
    halo_recv,
    out_sem,
):
    channels, samples = x.shape
    blocks = samples // BLOCK
    width = 8 * blocks
    row, column = lax.axis_index("tm"), lax.axis_index("chan")
    below, above = lax.rem(column + groups - 1, groups), lax.rem(column + 1, groups)

    loads = []
    for index, (source, target) in enumerate(
        (
            (mask_hbm, mask),
            (x_hbm, x),
            (first_hbm, first),
            (total_hbm, total),
            (across_hbm.at[row], across),
            (space_hbm, space),
            (states_hbm, states),
            (outer_hbm, outer),
            (inner_hbm, inner),
            (main_hbm, main),
            (correct_hbm, correct),
        )
    ):
        copy = pltpu.make_async_copy(source, target, load_sem.at[index])
        copy.start()
        loads.append(copy)

    barrier = pltpu.get_barrier_semaphore()
    for side in (below, above):
        pl.semaphore_signal(barrier, inc=1, device_id=(row, side), device_id_type=MESH)
    for step in range(1, devices):
        peer = lax.rem(row + step, devices)
        pl.semaphore_signal(barrier, inc=1, device_id=(peer, column), device_id_type=MESH)

    loads[0].wait()
    here = lax.broadcasted_iota(jnp.int32, (channels, channels), 0)
    there = lax.broadcasted_iota(jnp.int32, (channels, channels), 1)
    live = jnp.where(here == there, mask[...].astype(jnp.float32), 0.0)
    live = jnp.sum(live, axis=1, keepdims=True)
    loads[1].wait()
    x[...] = x[...] * live

    pl.semaphore_wait(barrier, devices + 1)

    length = samples // PIECES
    pieces = []
    for piece in range(PIECES):
        span = pl.ds(piece * length, length)
        pair = []
        for way, (side, source, target) in enumerate(
            ((above, channels - RADIUS, 0), (below, 0, RADIUS))
        ):
            copy = pltpu.make_async_remote_copy(
                src_ref=x.at[pl.ds(source, RADIUS), span],
                dst_ref=halo.at[pl.ds(target, RADIUS), span],
                send_sem=halo_send.at[way, piece],
                recv_sem=halo_recv.at[way, piece],
                device_id=(row, side),
                device_id_type=MESH,
            )
            copy.start()
            pair.append(copy)
        pieces.append(pair)

    slot = lax.broadcasted_iota(jnp.int32, (channels, width), 1) // 8

    def stacked(value):
        return jnp.concatenate(
            [value[:, k * BLOCK : (k + 1) * BLOCK] for k in range(value.shape[1] // BLOCK)], axis=0
        )

    def gathered(value, start):
        kept = [
            jnp.where(slot == start + k, value[k * channels : (k + 1) * channels], 0.0)
            for k in range(value.shape[0] // channels)
        ]
        return functools.reduce(jnp.add, kept)

    x_high, x_low = halves(x[...])
    s_high, s_low = stacked(x_high), stacked(x_low)
    loads[2].wait()
    loads[3].wait()
    given = gathered(
        jnp.dot(
            jnp.concatenate([s_high, s_low, s_high], axis=1),
            first[...],
            preferred_element_type=jnp.float32,
        ),
        0,
    )
    nt = (((1,), (1,)), ((), ()))
    mine = lax.dot_general(
        total[...], given, nt, precision=highest, preferred_element_type=jnp.float32
    )
    ends[row] = jnp.concatenate([mine, jnp.zeros((8, LANES - channels), jnp.float32)], axis=1)

    def end_copy(to, slot_index):
        return pltpu.make_async_remote_copy(
            src_ref=ends.at[slot_index],
            dst_ref=ends.at[slot_index],
            send_sem=end_send.at[to],
            recv_sem=end_recv.at[slot_index],
            device_id=(to, column),
            device_id_type=MESH,
        )

    sent = []
    for step in range(1, devices):
        copy = end_copy(lax.rem(row + step, devices), row)
        copy.start()
        sent.append(copy)
    for load in loads[4:]:
        load.wait()

    for step in range(1, devices):
        end_copy(row, lax.rem(row + step, devices)).wait_recv()
    entering[0] = jnp.dot(
        across[...],
        ends[...].reshape(devices * 8, LANES),
        precision=highest,
        preferred_element_type=jnp.float32,
    )
    near = []
    for way, side in enumerate((above, below)):
        copy = pltpu.make_async_remote_copy(
            src_ref=entering.at[0],
            dst_ref=entering.at[1 + way],
            send_sem=near_send.at[way],
            recv_sem=near_recv.at[way],
            device_id=(row, side),
            device_id_type=MESH,
        )
        copy.start()
        near.append(copy)

    has_below = jnp.where(column > 0, 1.0, 0.0).astype(jnp.float32)
    has_above = jnp.where(column < groups - 1, 1.0, 0.0).astype(jnp.float32)
    lane = lax.broadcasted_iota(jnp.int32, (channels, 6 * 2 * RADIUS), 1)
    part = lax.rem(lane, 2 * RADIUS)
    keep = jnp.where(lane >= 3 * 2 * RADIUS, 1.0, jnp.where(part < RADIUS, has_below, has_above))
    band = (space[...].astype(jnp.float32) * keep).astype(jnp.bfloat16)

    collected = jnp.zeros((channels, width), jnp.float32)
    per = length // BLOCK
    for piece in range(PIECES):
        for copy in pieces[piece]:
            copy.wait_recv()
        low, high = piece * length, (piece + 1) * length
        h_high, h_low = halves(halo[:, low:high])
        both = jnp.concatenate(
            [h_high, h_high, h_low, x_high[:, low:high], x_high[:, low:high], x_low[:, low:high]],
            axis=0,
        )
        mixed = jnp.dot(band, both, preferred_element_type=jnp.float32)
        m_high, m_low = halves(stacked(mixed))
        answer = jnp.dot(
            jnp.concatenate([m_high, m_low, m_high], axis=1),
            main[...],
            preferred_element_type=jnp.float32,
        )
        collected = collected + gathered(answer[:, :width], piece * per)
        plain[pl.ds(piece * per * channels, per * channels), :] = answer[:, width:]

    for copy in near:
        copy.wait_recv()
    lane = lax.broadcasted_iota(jnp.int32, (channels, 3 * LANES), 1)
    keep = jnp.where(
        lane < LANES, 1.0, jnp.where(lane < 2 * LANES, has_below, has_above)
    )
    outside = lax.dot_general(
        states[...] * keep,
        jnp.concatenate([entering[0], entering[1], entering[2]], axis=1),
        nt,
        precision=highest,
        preferred_element_type=jnp.float32,
    )
    taken = jnp.dot(
        collected, inner[...], precision=highest, preferred_element_type=jnp.float32
    ) + jnp.dot(outside, outer[...], precision=highest, preferred_element_type=jnp.float32)
    t_high, t_low = halves(taken)
    writes = []
    for piece in range(PIECES):
        rows = []
        for k in range(piece * per, (piece + 1) * per):
            chosen = slot == k
            k_high = jnp.where(chosen, t_high, jnp.zeros_like(t_high))
            k_low = jnp.where(chosen, t_low, jnp.zeros_like(t_low))
            rows.append(jnp.concatenate([k_high, k_low, k_high], axis=1))
        fixed = plain[pl.ds(piece * per * channels, per * channels), :] + jnp.dot(
            jnp.concatenate(rows, axis=0), correct[...], preferred_element_type=jnp.float32
        )
        for k in range(per):
            at = piece * length + k * BLOCK
            result[:, at : at + BLOCK] = fixed[k * channels : (k + 1) * channels]
        span = pl.ds(piece * length, length)
        copy = pltpu.make_async_copy(result.at[:, span], out_hbm.at[:, span], out_sem.at[piece])
        copy.start()
        writes.append(copy)

    for copy in sent + near + [copy for pair in pieces for copy in pair]:
        copy.wait_send()
    for copy in writes:
        copy.wait()


def shards(devices, groups, strain, channel_mask):
    channels, samples = strain.shape
    tables = filter_tables(samples // BLOCK, devices) + space_tables(channels)
    tables = [jnp.asarray(table) for table in tables]
    f32 = jnp.float32
    held = [pltpu.VMEM(table.shape, table.dtype) for table in tables]
    held[6] = pltpu.VMEM(tables[6].shape[1:], f32)
    return pl.pallas_call(
        functools.partial(kernel, devices, groups),
        out_shape=jax.ShapeDtypeStruct((channels, samples), f32),
        in_specs=[pl.BlockSpec(memory_space=pltpu.HBM)] * (2 + len(tables)),
        out_specs=pl.BlockSpec(memory_space=pl.ANY),
        scratch_shapes=[
            pltpu.VMEM((channels, samples), f32),
            pltpu.VMEM((1, channels), jnp.int32),
            *held,
            pltpu.VMEM((2 * RADIUS, samples), f32),
            pltpu.VMEM((devices, 8, LANES), f32),
            pltpu.VMEM((3, 8, LANES), f32),
            pltpu.VMEM((channels * samples // BLOCK, BLOCK), f32),
            pltpu.VMEM((channels, samples), f32),
            pltpu.SemaphoreType.DMA((2 + len(tables),)),
            pltpu.SemaphoreType.DMA((devices,)),
            pltpu.SemaphoreType.DMA((devices,)),
            pltpu.SemaphoreType.DMA((2,)),
            pltpu.SemaphoreType.DMA((2,)),
            pltpu.SemaphoreType.DMA((2, PIECES)),
            pltpu.SemaphoreType.DMA((2, PIECES)),
            pltpu.SemaphoreType.DMA((PIECES,)),
        ],
        compiler_params=pltpu.CompilerParams(
            collective_id=0, has_side_effects=True, vmem_limit_bytes=40 * 1024 * 1024
        ),
        name="bandpass",
    )(
        *[
            pltpu.with_memory_space_constraint(value, pltpu.HBM)
            for value in (strain, channel_mask.reshape(1, channels), *tables)
        ]
    )


def solution(mesh):
    placed = (P("chan", "tm"), P("chan"))
    sizes = dict(zip(mesh.axis_names, mesh.devices.shape))
    return jax.shard_map(
        functools.partial(shards, sizes["tm"], sizes["chan"]),
        mesh=mesh,
        in_specs=placed,
        out_specs=P("chan", "tm"),
        check_vma=False,
    )
```

```python
import functools
import math

import jax
import jax.numpy as jnp
import ml_dtypes
import numpy as np
from jax import lax
from jax.experimental import pallas as pl
from jax.experimental.pallas import tpu as pltpu
from jax.sharding import PartitionSpec as P

RADIUS = 16
BLOCK = 256
LANES = 128
PIECES = 4
EARLY = 2

low_corner = 0.015
high_corner = 100.0
sample_rate = 500.0
highest = lax.Precision.HIGHEST
MESH = pl.DeviceIdType.MESH


def section(corner, highpass):
    warped = 2.0 * sample_rate * math.tan(math.pi * corner / sample_rate)
    scaled = warped / (2.0 * sample_rate * math.sqrt(2.0))
    numer_real = 1.0 - scaled
    denom_real = 1.0 + scaled
    denom_imag = -scaled
    modulus = denom_real * denom_real + denom_imag * denom_imag
    pole_real = (numer_real * denom_real + scaled * denom_imag) / modulus
    pole_imag = (scaled * denom_real - numer_real * denom_imag) / modulus
    pole_norm = pole_real * pole_real + pole_imag * pole_imag
    zero_place = 1.0 if highpass else -1.0
    section_gain = ((1.0 + zero_place * pole_real) ** 2 + pole_imag * pole_imag) / 4.0
    linear = section_gain * (2.0 * pole_real - 2.0 * zero_place)
    constant = section_gain * (1.0 - pole_norm)
    shrink = 1.0 - math.sqrt(pole_norm)
    first_out = linear / shrink
    second = (constant + pole_real * linear) / (pole_imag * shrink)
    rotation = np.array([[pole_real, -pole_imag], [pole_imag, pole_real]])
    inject = np.array([shrink, 0.0])
    return (rotation, inject, np.array([first_out, second]), section_gain)


def filter_system():
    high_rotation, high_inject, high_out, high_gain = section(low_corner, True)
    low_rotation, low_inject, low_out, low_gain = section(high_corner, False)
    upper_rows = np.concatenate([high_rotation, np.zeros((2, 2))], axis=1)
    lower_rows = np.concatenate([np.outer(low_inject, high_out), low_rotation], axis=1)
    transition = np.concatenate([upper_rows, lower_rows], axis=0)
    driving = np.concatenate([high_inject, low_inject * high_gain])
    readout = np.concatenate([high_out * low_gain, low_out])
    direct = low_gain * high_gain
    return (transition, driving, readout, direct)


def spatial_taps(extent):
    positions = np.arange(-extent, extent + 1)
    window = 0.5 * (1.0 + np.cos(np.pi * positions / (extent + 1)))
    window = window / np.sum(window)
    return np.where(positions == 0, 1.0 - window, -window)


def chain(count, power, couple):
    powers = [np.eye(4)]
    for _ in range(count):
        powers.append(powers[-1] @ power)
    ahead = np.zeros((count, 4, count, 8))
    behind = np.zeros((count, 4, count, 8))
    for at in range(count):
        for other in range(at):
            ahead[at, :, other, :4] = powers[at - 1 - other]
    for at in range(count):
        for other in range(at + 1, count):
            gives = np.einsum("pq,qjr->pjr", couple, ahead[other])
            gives[:, other, 4:] += np.eye(4)
            behind[at] += np.einsum("pq,qjr->pjr", powers[other - 1 - at], gives)
    inner = np.concatenate([ahead, behind], axis=1)
    outer = np.zeros((count, 8, 8))
    for at in range(count):
        outer[at, :4, :4] = powers[at]
    for at in range(count):
        outer[at, 4:, 4:] = powers[count - 1 - at]
        for other in range(at + 1, count):
            outer[at, 4:, :4] += powers[other - 1 - at] @ couple @ outer[other, :4, :4]
    total = np.zeros((8, count, 8))
    for other in range(count):
        total[:4, other, :4] = powers[count - 1 - other]
        gives = np.einsum("pq,qjr->pjr", couple, ahead[other])
        gives[:, other, 4:] += np.eye(4)
        total[4:] += np.einsum("pq,qjr->pjr", powers[other], gives)
    pull = sum(powers[other] @ couple @ powers[other] for other in range(count))
    return inner, outer, total, powers[count], pull


def split(table):
    high = np.asarray(table, np.float32).astype(ml_dtypes.bfloat16)
    low = (np.asarray(table, np.float64) - high.astype(np.float64)).astype(np.float32)
    return high, low.astype(ml_dtypes.bfloat16)


def thrice(table):
    high, low = split(table)
    return np.concatenate([high, high, low], axis=0)


@functools.lru_cache(maxsize=None)
def filter_tables(blocks, devices):
    transition, driving, readout, direct = filter_system()
    powers = [np.eye(4)]
    for _ in range(BLOCK):
        powers.append(powers[-1] @ transition)
    response = np.array([direct] + [readout @ powers[lag] @ driving for lag in range(BLOCK - 1)])
    lag = np.arange(BLOCK)[:, None] - np.arange(BLOCK)[None, :]
    forward = np.where(lag >= 0, response[np.clip(lag, 0, BLOCK - 1)], 0.0)
    observe = np.stack([readout @ powers[at] for at in range(BLOCK)])
    reach = np.stack([powers[BLOCK - 1 - at] @ driving for at in range(BLOCK)], axis=1)
    both_ways = forward.T @ forward
    gives = np.concatenate([reach, reach[:, ::-1] @ forward], axis=0)
    takes = np.concatenate([forward.T @ observe, observe[::-1]], axis=1)
    couple = reach[:, ::-1] @ observe
    inner, outer, total, power, pull = chain(blocks, powers[BLOCK], couple)
    across = chain(devices, power, pull)[0]
    width = 8 * blocks
    main = thrice(np.concatenate([np.tile(gives.T, (1, blocks)), both_ways], axis=1))
    correct = thrice(np.tile(takes.T, (blocks, 1)))
    outside = thrice(np.concatenate([(takes @ outer[at]).T for at in range(blocks)], axis=1))
    gathers = across.reshape(devices, 8, devices, 4, 2).transpose(0, 3, 1, 2, 4)
    return (
        main,
        np.asarray(total.reshape(8, width), np.float32),
        np.asarray(inner.reshape(width, width).T, np.float32),
        correct,
        np.asarray(gathers.reshape(devices, 32, 2 * devices), np.float32),
        outside,
    )


@functools.lru_cache(maxsize=None)
def space_tables(channels):
    taps = spatial_taps(RADIUS)

    def band(sources):
        lag = np.asarray(sources)[None, :] - np.arange(channels)[:, None] + RADIUS
        inside = (lag >= 0) & (lag <= 2 * RADIUS)
        return np.where(inside, taps[np.clip(lag, 0, 2 * RADIUS)], 0.0)

    own = band(np.arange(channels))
    edge = np.concatenate(
        [band(np.arange(-RADIUS, 0)), band(np.arange(channels, channels + RADIUS))], axis=1
    )
    parts = []
    for table in (edge, own):
        high, low = split(table)
        parts.append(np.concatenate([high, low, high], axis=1))
    states = np.zeros((channels, 3 * LANES))
    states[:, :channels] = own
    states[:, LANES : LANES + channels] = band(np.arange(-channels, 0))
    states[:, 2 * LANES : 2 * LANES + channels] = band(np.arange(channels, 2 * channels))
    return parts[0], parts[1], np.asarray(states, np.float32)


def halves(value):
    high = value.astype(jnp.bfloat16)
    return high, (value - high.astype(jnp.float32)).astype(jnp.bfloat16)


def product(left, right):
    return jnp.dot(left, right, preferred_element_type=jnp.float32)


def exact(left, right):
    return jnp.dot(left, right, precision=highest, preferred_element_type=jnp.float32)


def exact_turned(left, right):
    turned = (((1,), (1,)), ((), ()))
    return lax.dot_general(
        left, right, turned, precision=highest, preferred_element_type=jnp.float32
    )


def kernel(
    devices,
    groups,
    x_hbm,
    mask_hbm,
    main_hbm,
    total_hbm,
    inner_hbm,
    correct_hbm,
    across_hbm,
    outside_hbm,
    edge_hbm,
    own_hbm,
    states_hbm,
    out,
    x,
    mask,
    main,
    total,
    inner,
    correct,
    across,
    outside,
    edge,
    own,
    states,
    halo,
    ends,
    entering,
    load_sem,
    end_send,
    end_recv,
    near_send,
    near_recv,
    halo_send,
    halo_recv,
):
    channels, samples = x.shape
    blocks = samples // BLOCK
    width = 8 * blocks
    row, column = lax.axis_index("tm"), lax.axis_index("chan")
    below, above = lax.rem(column + groups - 1, groups), lax.rem(column + 1, groups)
    up = (above, column < groups - 1, column > 0)
    down = (below, column > 0, column < groups - 1)
    half = devices // 2
    order = sorted(range(1, devices), key=lambda step: abs(step - half))

    barrier = pltpu.get_barrier_semaphore()
    for step in order:
        peer = lax.rem(row + step, devices)
        pl.semaphore_signal(barrier, inc=1, device_id=(peer, column), device_id_type=MESH)
    for side, sends, gets in (up, down):

        @pl.when(sends)
        def _():
            pl.semaphore_signal(barrier, inc=1, device_id=(row, side), device_id_type=MESH)

    loads = []
    for index, (source, target) in enumerate(
        (
            (mask_hbm, mask),
            (x_hbm, x),
            (main_hbm, main),
            (total_hbm, total),
            (inner_hbm, inner),
            (correct_hbm, correct),
            (across_hbm.at[row], across),
            (own_hbm, own),
            (edge_hbm, edge),
            (states_hbm, states),
            (outside_hbm, outside),
        )
    ):
        copy = pltpu.make_async_copy(source, target, load_sem.at[index])
        copy.start()
        loads.append(copy)

    @pl.when(column == 0)
    def _():
        halo[pl.ds(0, RADIUS), :] = jnp.zeros((RADIUS, samples), jnp.float32)
        entering[1] = jnp.zeros((8, LANES), jnp.float32)

    @pl.when(column == groups - 1)
    def _():
        halo[pl.ds(RADIUS, RADIUS), :] = jnp.zeros((RADIUS, samples), jnp.float32)
        entering[2] = jnp.zeros((8, LANES), jnp.float32)

    loads[0].wait()
    here = lax.broadcasted_iota(jnp.int32, (channels, channels), 0)
    there = lax.broadcasted_iota(jnp.int32, (channels, channels), 1)
    live = jnp.where(here == there, mask[...].astype(jnp.float32), 0.0)
    live = jnp.sum(live, axis=1, keepdims=True)
    loads[1].wait()
    high, low = halves(
        jnp.concatenate(
            [x[:, k * BLOCK : (k + 1) * BLOCK] * live for k in range(blocks)], axis=0
        )
    )
    loads[2].wait()
    answer = product(jnp.concatenate([high, low, high], axis=1), main[...])
    slot = lax.broadcasted_iota(jnp.int32, (channels, width), 1) // 8
    given = functools.reduce(
        jnp.add,
        [
            jnp.where(slot == k, answer[k * channels : (k + 1) * channels, :width], 0.0)
            for k in range(blocks)
        ],
    )
    for load in loads[3:]:
        load.wait()
    mine = exact_turned(total[...], given)
    entering[0] = jnp.concatenate([mine, jnp.zeros((8, LANES - channels), jnp.float32)], axis=1)
    high, low = halves(exact(given, inner[...]))
    rows = []
    for k in range(blocks):
        k_high = jnp.where(slot == k, high, jnp.zeros_like(high))
        k_low = jnp.where(slot == k, low, jnp.zeros_like(low))
        rows.append(jnp.concatenate([k_high, k_low, k_high], axis=1))
    local = answer[:, width:] + product(jnp.concatenate(rows, axis=0), correct[...])
    for k in range(blocks):
        x[:, k * BLOCK : (k + 1) * BLOCK] = local[k * channels : (k + 1) * channels]

    others = jnp.where(column > 0, 1, 0) + jnp.where(column < groups - 1, 1, 0)
    pl.semaphore_wait(barrier, devices - 1 + others)

    near = []
    for way, (side, sends, gets) in enumerate((up, down)):
        copy = pltpu.make_async_remote_copy(
            src_ref=entering.at[0],
            dst_ref=entering.at[1 + way],
            send_sem=near_send.at[way],
            recv_sem=near_recv.at[way],
            device_id=(row, side),
            device_id_type=MESH,
        )
        pl.when(sends)(copy.start)
        near.append((copy, sends, gets))

    length = samples // PIECES
    pieces = []
    for piece in range(PIECES):
        span = pl.ds(piece * length, length)
        pair = []
        for way, ((side, sends, gets), source, target) in enumerate(
            ((up, channels - RADIUS, 0), (down, 0, RADIUS))
        ):
            copy = pltpu.make_async_remote_copy(
                src_ref=x.at[pl.ds(source, RADIUS), span],
                dst_ref=halo.at[pl.ds(target, RADIUS), span],
                send_sem=halo_send.at[way, piece],
                recv_sem=halo_recv.at[way, piece],
                device_id=(row, side),
                device_id_type=MESH,
            )
            pl.when(sends)(copy.start)
            pair.append((copy, sends, gets))
        pieces.append(pair)

    high, low = halves(x[...])
    out[...] = product(own[...], jnp.concatenate([high, high, low], axis=0))

    def receive(piece):
        for copy, sends, gets in pieces[piece]:
            pl.when(gets)(copy.wait_recv)
        begin, end = piece * length, (piece + 1) * length
        high, low = halves(halo[:, begin:end])
        out[:, begin:end] += product(edge[...], jnp.concatenate([high, high, low], axis=0))

    for copy, sends, gets in near:
        pl.when(gets)(copy.wait_recv)
    mine = exact_turned(
        jnp.concatenate([entering[0], entering[1], entering[2]], axis=1), states[...]
    )
    ends[row] = jnp.concatenate([mine[2 * k : 2 * k + 2] for k in range(4)], axis=1)

    def end_copy(to, slot_index):
        return pltpu.make_async_remote_copy(
            src_ref=ends.at[slot_index],
            dst_ref=ends.at[slot_index],
            send_sem=end_send.at[to],
            recv_sem=end_recv.at[slot_index],
            device_id=(to, column),
            device_id_type=MESH,
        )

    sent = []
    for step in order:
        copy = end_copy(lax.rem(row + step, devices), row)
        copy.start()
        sent.append(copy)

    for piece in range(EARLY):
        receive(piece)

    for step in reversed(order):
        end_copy(row, lax.rem(row + step, devices)).wait_recv()
    packed = jnp.concatenate([ends[k] for k in range(devices)], axis=0)
    mixed = exact(across[...], packed)
    taken = mixed[0:8, :channels] + functools.reduce(
        jnp.add,
        [
            pltpu.roll(mixed[8 * k : 8 * k + 8], LANES - 32 * k, axis=1)[:, :channels]
            for k in range(1, 4)
        ],
    )

    for piece in range(EARLY, PIECES):
        receive(piece)

    high, low = halves(taken)
    out[...] += lax.dot_general(
        jnp.concatenate([high, low, high], axis=0),
        outside[...],
        (((0,), (0,)), ((), ())),
        preferred_element_type=jnp.float32,
    )

    for copy in sent:
        copy.wait_send()
    for copy, sends, gets in near + [copy for pair in pieces for copy in pair]:
        pl.when(sends)(copy.wait_send)


def shards(devices, groups, strain, channel_mask):
    channels, samples = strain.shape
    tables = filter_tables(samples // BLOCK, devices) + space_tables(channels)
    tables = [jnp.asarray(table) for table in tables]
    f32 = jnp.float32
    held = [pltpu.VMEM(table.shape, table.dtype) for table in tables]
    held[4] = pltpu.VMEM(tables[4].shape[1:], f32)
    return pl.pallas_call(
        functools.partial(kernel, devices, groups),
        out_shape=jax.ShapeDtypeStruct((channels, samples), f32),
        in_specs=[pl.BlockSpec(memory_space=pltpu.HBM)] * (2 + len(tables)),
        out_specs=pl.BlockSpec(memory_space=pltpu.VMEM),
        scratch_shapes=[
            pltpu.VMEM((channels, samples), f32),
            pltpu.VMEM((1, channels), jnp.int32),
            *held,
            pltpu.VMEM((2 * RADIUS, samples), f32),
            pltpu.VMEM((devices, 2, LANES), f32),
            pltpu.VMEM((3, 8, LANES), f32),
            pltpu.SemaphoreType.DMA((2 + len(tables),)),
            pltpu.SemaphoreType.DMA((devices,)),
            pltpu.SemaphoreType.DMA((devices,)),
            pltpu.SemaphoreType.DMA((2,)),
            pltpu.SemaphoreType.DMA((2,)),
            pltpu.SemaphoreType.DMA((2, PIECES)),
            pltpu.SemaphoreType.DMA((2, PIECES)),
        ],
        compiler_params=pltpu.CompilerParams(
            collective_id=0, has_side_effects=True, vmem_limit_bytes=40 * 1024 * 1024
        ),
        name="bandpass",
    )(
        *[
            pltpu.with_memory_space_constraint(value, pltpu.HBM)
            for value in (strain, channel_mask.reshape(1, channels), *tables)
        ]
    )


def solution(mesh):
    placed = (P("chan", "tm"), P("chan"))
    sizes = dict(zip(mesh.axis_names, mesh.devices.shape))
    return jax.shard_map(
        functools.partial(shards, sizes["tm"], sizes["chan"]),
        mesh=mesh,
        in_specs=placed,
        out_specs=P("chan", "tm"),
        check_vma=False,
    )
```

```python
import functools
import math

import jax
import jax.numpy as jnp
import ml_dtypes
import numpy as np
from jax import lax
from jax.experimental import pallas as pl
from jax.experimental.pallas import tpu as pltpu
from jax.sharding import PartitionSpec as P

RADIUS = 16
BLOCK = 256
LANES = 128
PIECES = 4
EARLY = 3

low_corner = 0.015
high_corner = 100.0
sample_rate = 500.0
MESH = pl.DeviceIdType.MESH


def section(corner, highpass):
    warped = 2.0 * sample_rate * math.tan(math.pi * corner / sample_rate)
    scaled = warped / (2.0 * sample_rate * math.sqrt(2.0))
    numer_real = 1.0 - scaled
    denom_real = 1.0 + scaled
    denom_imag = -scaled
    modulus = denom_real * denom_real + denom_imag * denom_imag
    pole_real = (numer_real * denom_real + scaled * denom_imag) / modulus
    pole_imag = (scaled * denom_real - numer_real * denom_imag) / modulus
    pole_norm = pole_real * pole_real + pole_imag * pole_imag
    zero_place = 1.0 if highpass else -1.0
    section_gain = ((1.0 + zero_place * pole_real) ** 2 + pole_imag * pole_imag) / 4.0
    linear = section_gain * (2.0 * pole_real - 2.0 * zero_place)
    constant = section_gain * (1.0 - pole_norm)
    shrink = 1.0 - math.sqrt(pole_norm)
    first_out = linear / shrink
    second = (constant + pole_real * linear) / (pole_imag * shrink)
    rotation = np.array([[pole_real, -pole_imag], [pole_imag, pole_real]])
    inject = np.array([shrink, 0.0])
    return (rotation, inject, np.array([first_out, second]), section_gain)


def filter_system():
    high_rotation, high_inject, high_out, high_gain = section(low_corner, True)
    low_rotation, low_inject, low_out, low_gain = section(high_corner, False)
    upper_rows = np.concatenate([high_rotation, np.zeros((2, 2))], axis=1)
    lower_rows = np.concatenate([np.outer(low_inject, high_out), low_rotation], axis=1)
    transition = np.concatenate([upper_rows, lower_rows], axis=0)
    driving = np.concatenate([high_inject, low_inject * high_gain])
    readout = np.concatenate([high_out * low_gain, low_out])
    direct = low_gain * high_gain
    return (transition, driving, readout, direct)


def spatial_taps(extent):
    positions = np.arange(-extent, extent + 1)
    window = 0.5 * (1.0 + np.cos(np.pi * positions / (extent + 1)))
    window = window / np.sum(window)
    return np.where(positions == 0, 1.0 - window, -window)


def chain(count, power, couple):
    powers = [np.eye(4)]
    for _ in range(count):
        powers.append(powers[-1] @ power)
    ahead = np.zeros((count, 4, count, 8))
    behind = np.zeros((count, 4, count, 8))
    for at in range(count):
        for other in range(at):
            ahead[at, :, other, :4] = powers[at - 1 - other]
    for at in range(count):
        for other in range(at + 1, count):
            gives = np.einsum("pq,qjr->pjr", couple, ahead[other])
            gives[:, other, 4:] += np.eye(4)
            behind[at] += np.einsum("pq,qjr->pjr", powers[other - 1 - at], gives)
    inner = np.concatenate([ahead, behind], axis=1)
    outer = np.zeros((count, 8, 8))
    for at in range(count):
        outer[at, :4, :4] = powers[at]
    for at in range(count):
        outer[at, 4:, 4:] = powers[count - 1 - at]
        for other in range(at + 1, count):
            outer[at, 4:, :4] += powers[other - 1 - at] @ couple @ outer[other, :4, :4]
    total = np.zeros((8, count, 8))
    for other in range(count):
        total[:4, other, :4] = powers[count - 1 - other]
        gives = np.einsum("pq,qjr->pjr", couple, ahead[other])
        gives[:, other, 4:] += np.eye(4)
        total[4:] += np.einsum("pq,qjr->pjr", powers[other], gives)
    pull = sum(powers[other] @ couple @ powers[other] for other in range(count))
    return inner, outer, total, powers[count], pull


def split(table):
    high = np.asarray(table, np.float32).astype(ml_dtypes.bfloat16)
    low = (np.asarray(table, np.float64) - high.astype(np.float64)).astype(np.float32)
    return high, low.astype(ml_dtypes.bfloat16)


def thrice(table):
    high, low = split(table)
    return np.concatenate([high, high, low], axis=0)


def beside(table):
    high, low = split(table)
    return np.concatenate([high, high, low], axis=1)


@functools.lru_cache(maxsize=None)
def filter_tables(blocks, devices):
    transition, driving, readout, direct = filter_system()
    powers = [np.eye(4)]
    for _ in range(BLOCK):
        powers.append(powers[-1] @ transition)
    response = np.array([direct] + [readout @ powers[lag] @ driving for lag in range(BLOCK - 1)])
    lag = np.arange(BLOCK)[:, None] - np.arange(BLOCK)[None, :]
    forward = np.where(lag >= 0, response[np.clip(lag, 0, BLOCK - 1)], 0.0)
    observe = np.stack([readout @ powers[at] for at in range(BLOCK)])
    reach = np.stack([powers[BLOCK - 1 - at] @ driving for at in range(BLOCK)], axis=1)
    both_ways = forward.T @ forward
    gives = np.concatenate([reach, reach[:, ::-1] @ forward], axis=0)
    takes = np.concatenate([forward.T @ observe, observe[::-1]], axis=1)
    couple = reach[:, ::-1] @ observe
    inner, outer, total, power, pull = chain(blocks, powers[BLOCK], couple)
    across = chain(devices, power, pull)[0]
    width = 8 * blocks
    first = thrice(np.tile(gives.T, (1, blocks)))
    main = thrice(both_ways)
    correct = thrice(np.tile(takes.T, (blocks, 1)))
    outside = thrice(np.concatenate([(takes @ outer[at]).T for at in range(blocks)], axis=1))
    gathers = across.reshape(devices, 8, devices, 4, 2).transpose(0, 3, 1, 2, 4)
    gathers = gathers.reshape(devices, 32, 2 * devices)
    return (
        first,
        beside(total.reshape(8, width)),
        main,
        thrice(inner.reshape(width, width).T),
        correct,
        np.stack([beside(gathers[at]) for at in range(devices)]),
        outside,
    )


@functools.lru_cache(maxsize=None)
def space_tables(channels):
    taps = spatial_taps(RADIUS)

    def band(sources):
        lag = np.asarray(sources)[None, :] - np.arange(channels)[:, None] + RADIUS
        inside = (lag >= 0) & (lag <= 2 * RADIUS)
        return np.where(inside, taps[np.clip(lag, 0, 2 * RADIUS)], 0.0)

    own = band(np.arange(channels))
    edge = np.concatenate(
        [band(np.arange(-RADIUS, 0)), band(np.arange(channels, channels + RADIUS))], axis=1
    )
    parts = []
    for table in (edge, own):
        high, low = split(table)
        parts.append(np.concatenate([high, low, high], axis=1))
    states = np.zeros((channels, 3 * LANES))
    states[:, :channels] = own
    states[:, LANES : LANES + channels] = band(np.arange(-channels, 0))
    states[:, 2 * LANES : 2 * LANES + channels] = band(np.arange(channels, 2 * channels))
    return parts[0], parts[1], beside(states)


def halves(value):
    high = value.astype(jnp.bfloat16)
    return high, (value - high.astype(jnp.float32)).astype(jnp.bfloat16)


def product(left, right):
    return jnp.dot(left, right, preferred_element_type=jnp.float32)


def product_turned(left, right):
    turned = (((1,), (1,)), ((), ()))
    return lax.dot_general(left, right, turned, preferred_element_type=jnp.float32)


def tripled(value, axis):
    high, low = halves(value)
    return jnp.concatenate([high, low, high], axis=axis)


def kernel(
    devices,
    groups,
    x_hbm,
    mask_hbm,
    first_hbm,
    total_hbm,
    main_hbm,
    inner_hbm,
    correct_hbm,
    across_hbm,
    outside_hbm,
    edge_hbm,
    own_hbm,
    states_hbm,
    out,
    x,
    mask,
    first,
    total,
    main,
    inner,
    correct,
    across,
    outside,
    edge,
    own,
    states,
    halo,
    ends,
    entering,
    parts,
    load_sem,
    x_sem,
    end_send,
    end_recv,
    near_send,
    near_recv,
    halo_send,
    halo_recv,
    relay_sem,
):
    channels, samples = x.shape
    blocks = samples // BLOCK
    width = 8 * blocks
    row, column = lax.axis_index("tm"), lax.axis_index("chan")
    below, above = lax.rem(column + groups - 1, groups), lax.rem(column + 1, groups)
    up = (above, column < groups - 1, column > 0)
    down = (below, column > 0, column < groups - 1)
    half = devices // 2
    order = sorted(range(1, devices), key=lambda step: abs(step - half))

    reach = -(-half // 4)
    steps = sorted({hop % half for hop in range(-reach, reach + 1)} - {0})
    relays = sorted({reach % half, -reach % half} - {0})
    chip, core = row // 2, row % 2
    greeted = [lax.rem(chip + hop, half) * 2 + core for hop in steps]
    greeted += [lax.rem(chip + hop, half) * 2 + 1 - core for hop in [*steps, 0]]

    quarter = samples // PIECES
    arrivals = []
    for piece in range(PIECES):
        span = pl.ds(piece * quarter, quarter)
        arrivals.append(pltpu.make_async_copy(x_hbm.at[:, span], x.at[:, span], x_sem.at[piece]))
    loads = []
    for index, (source, target) in enumerate(
        (
            (mask_hbm, mask),
            (first_hbm, first),
            (total_hbm, total),
            (main_hbm, main),
            (inner_hbm, inner),
            (correct_hbm, correct),
            (states_hbm, states),
            (across_hbm.at[row], across),
            (own_hbm, own),
            (edge_hbm, edge),
            (outside_hbm, outside),
        )
    ):
        loads.append(pltpu.make_async_copy(source, target, load_sem.at[index]))
    for copy in (*arrivals, *loads[:3]):
        copy.start()

    barrier = pltpu.get_barrier_semaphore()
    for peer in greeted:
        pl.semaphore_signal(barrier, inc=1, device_id=(peer, column), device_id_type=MESH)
    for side, sends, gets in (up, down):

        @pl.when(sends)
        def _():
            pl.semaphore_signal(barrier, inc=1, device_id=(row, side), device_id_type=MESH)

    for copy in loads[3:]:
        copy.start()

    @pl.when(column == 0)
    def _():
        halo[pl.ds(0, RADIUS), :] = jnp.zeros((RADIUS, samples), jnp.float32)
        entering[1] = jnp.zeros((8, LANES), jnp.float32)

    @pl.when(column == groups - 1)
    def _():
        halo[pl.ds(RADIUS, RADIUS), :] = jnp.zeros((RADIUS, samples), jnp.float32)
        entering[2] = jnp.zeros((8, LANES), jnp.float32)

    loads[0].wait()
    here = lax.broadcasted_iota(jnp.int32, (channels, channels), 0)
    there = lax.broadcasted_iota(jnp.int32, (channels, channels), 1)
    live = jnp.where(here == there, mask[...].astype(jnp.float32), 0.0)
    live = jnp.sum(live, axis=1, keepdims=True)
    slot = lax.broadcasted_iota(jnp.int32, (channels, width), 1) // 8
    per = quarter // BLOCK
    given = jnp.zeros((channels, width), jnp.float32)
    for piece in range(PIECES):
        arrivals[piece].wait()
        at = [(piece * per + k) * BLOCK for k in range(per)]
        value = jnp.concatenate([x[:, k : k + BLOCK] * live for k in at], axis=0)
        triple = tripled(value, 1)
        size = per * channels
        parts[piece * size : (piece + 1) * size, :] = triple
        if piece == 0:
            loads[1].wait()
        answer = product(triple, first[...])
        for k in range(per):
            mine = answer[k * channels : (k + 1) * channels]
            given = given + jnp.where(slot == piece * per + k, mine, 0.0)
    given = tripled(given, 1)
    loads[2].wait()
    mine = product_turned(total[...], given)
    entering[0] = jnp.concatenate([mine, jnp.zeros((8, LANES - channels), jnp.float32)], axis=1)

    def finish():
        for load in loads[3:6]:
            load.wait()
        high, low = halves(product(given, inner[...]))
        rows = []
        for k in range(blocks):
            k_high = jnp.where(slot == k, high, jnp.zeros_like(high))
            k_low = jnp.where(slot == k, low, jnp.zeros_like(low))
            rows.append(jnp.concatenate([k_high, k_low, k_high], axis=1))
        local = product(parts[...], main[...]) + product(
            jnp.concatenate(rows, axis=0), correct[...]
        )
        for k in range(blocks):
            x[:, k * BLOCK : (k + 1) * BLOCK] = local[k * channels : (k + 1) * channels]

    early = chip < half // 2
    pl.when(early)(finish)

    others = jnp.where(column > 0, 1, 0) + jnp.where(column < groups - 1, 1, 0)
    pl.semaphore_wait(barrier, len(greeted) + others)
    for hop in relays:
        peer = lax.rem(chip + hop, half) * 2 + core
        pl.semaphore_signal(relay_sem, inc=1, device_id=(peer, column), device_id_type=MESH)

    near = []
    for way, (side, sends, gets) in enumerate((up, down)):
        copy = pltpu.make_async_remote_copy(
            src_ref=entering.at[0],
            dst_ref=entering.at[1 + way],
            send_sem=near_send.at[way],
            recv_sem=near_recv.at[way],
            device_id=(row, side),
            device_id_type=MESH,
        )
        pl.when(sends)(copy.start)
        near.append((copy, sends, gets))

    pl.when(jnp.logical_not(early))(finish)
    for load in loads[6:]:
        load.wait()

    length = samples // PIECES
    pieces = []
    for piece in range(PIECES):
        span = pl.ds(piece * length, length)
        pair = []
        for way, ((side, sends, gets), source, target) in enumerate(
            ((up, channels - RADIUS, 0), (down, 0, RADIUS))
        ):
            copy = pltpu.make_async_remote_copy(
                src_ref=x.at[pl.ds(source, RADIUS), span],
                dst_ref=halo.at[pl.ds(target, RADIUS), span],
                send_sem=halo_send.at[way, piece],
                recv_sem=halo_recv.at[way, piece],
                device_id=(row, side),
                device_id_type=MESH,
            )
            pl.when(sends)(copy.start)
            pair.append((copy, sends, gets))
        pieces.append(pair)

    high, low = halves(x[...])
    out[...] = product(own[...], jnp.concatenate([high, high, low], axis=0))

    def receive(piece):
        for copy, sends, gets in pieces[piece]:
            pl.when(gets)(copy.wait_recv)
        begin, end = piece * length, (piece + 1) * length
        high, low = halves(halo[:, begin:end])
        out[:, begin:end] += product(edge[...], jnp.concatenate([high, high, low], axis=0))

    for copy, sends, gets in near:
        pl.when(gets)(copy.wait_recv)
    mine = product_turned(
        tripled(jnp.concatenate([entering[0], entering[1], entering[2]], axis=1), 1), states[...]
    )
    ends[row] = jnp.concatenate([mine[2 * k : 2 * k + 2] for k in range(4)], axis=1)

    def end_copy(to, slot_index):
        return pltpu.make_async_remote_copy(
            src_ref=ends.at[slot_index],
            dst_ref=ends.at[slot_index],
            send_sem=end_send.at[to],
            recv_sem=end_recv.at[slot_index],
            device_id=(to, column),
            device_id_type=MESH,
        )

    if relays:
        pl.semaphore_wait(relay_sem, len(relays))
    sent = []
    for step in order:
        copy = end_copy(lax.rem(row + step, devices), row)
        copy.start()
        sent.append(copy)

    for piece in range(EARLY):
        receive(piece)

    for step in reversed(order):
        end_copy(row, lax.rem(row + step, devices)).wait_recv()
    packed = jnp.concatenate([ends[k] for k in range(devices)], axis=0)
    mixed = product(across[...], tripled(packed, 0))
    taken = mixed[0:8, :channels] + functools.reduce(
        jnp.add,
        [
            pltpu.roll(mixed[8 * k : 8 * k + 8], LANES - 32 * k, axis=1)[:, :channels]
            for k in range(1, 4)
        ],
    )

    for piece in range(EARLY, PIECES):
        receive(piece)

    out[...] += lax.dot_general(
        tripled(taken, 0),
        outside[...],
        (((0,), (0,)), ((), ())),
        preferred_element_type=jnp.float32,
    )

    for copy in sent:
        copy.wait_send()
    for copy, sends, gets in near + [copy for pair in pieces for copy in pair]:
        pl.when(sends)(copy.wait_send)


def shards(devices, groups, strain, channel_mask):
    channels, samples = strain.shape
    tables = filter_tables(samples // BLOCK, devices) + space_tables(channels)
    tables = [jnp.asarray(table) for table in tables]
    f32 = jnp.float32
    held = [pltpu.VMEM(table.shape, table.dtype) for table in tables]
    held[5] = pltpu.VMEM(tables[5].shape[1:], tables[5].dtype)
    return pl.pallas_call(
        functools.partial(kernel, devices, groups),
        out_shape=jax.ShapeDtypeStruct((channels, samples), f32),
        in_specs=[pl.BlockSpec(memory_space=pltpu.HBM)] * (2 + len(tables)),
        out_specs=pl.BlockSpec(memory_space=pltpu.VMEM),
        scratch_shapes=[
            pltpu.VMEM((channels, samples), f32),
            pltpu.VMEM((1, channels), jnp.int32),
            *held,
            pltpu.VMEM((2 * RADIUS, samples), f32),
            pltpu.VMEM((devices, 2, LANES), f32),
            pltpu.VMEM((3, 8, LANES), f32),
            pltpu.VMEM((channels * samples // BLOCK, 3 * BLOCK), jnp.bfloat16),
            pltpu.SemaphoreType.DMA((2 + len(tables),)),
            pltpu.SemaphoreType.DMA((PIECES,)),
            pltpu.SemaphoreType.DMA((devices,)),
            pltpu.SemaphoreType.DMA((devices,)),
            pltpu.SemaphoreType.DMA((2,)),
            pltpu.SemaphoreType.DMA((2,)),
            pltpu.SemaphoreType.DMA((2, PIECES)),
            pltpu.SemaphoreType.DMA((2, PIECES)),
            pltpu.SemaphoreType.REGULAR,
        ],
        compiler_params=pltpu.CompilerParams(
            collective_id=0, has_side_effects=True, vmem_limit_bytes=40 * 1024 * 1024
        ),
        name="bandpass",
    )(
        *[
            pltpu.with_memory_space_constraint(value, pltpu.HBM)
            for value in (strain, channel_mask.reshape(1, channels), *tables)
        ]
    )


def solution(mesh):
    placed = (P("chan", "tm"), P("chan"))
    sizes = dict(zip(mesh.axis_names, mesh.devices.shape))
    return jax.shard_map(
        functools.partial(shards, sizes["tm"], sizes["chan"]),
        mesh=mesh,
        in_specs=placed,
        out_specs=P("chan", "tm"),
        check_vma=False,
    )
```

```python
import functools
import math

import jax
import jax.numpy as jnp
import ml_dtypes
import numpy as np
from jax import lax
from jax.experimental import pallas as pl
from jax.experimental.pallas import tpu as pltpu
from jax.sharding import PartitionSpec as P

RADIUS = 16
BLOCK = 256
LANES = 128
PIECES = 4
EARLY = 3

low_corner = 0.015
high_corner = 100.0
sample_rate = 500.0
MESH = pl.DeviceIdType.MESH


def section(corner, highpass):
    warped = 2.0 * sample_rate * math.tan(math.pi * corner / sample_rate)
    scaled = warped / (2.0 * sample_rate * math.sqrt(2.0))
    numer_real = 1.0 - scaled
    denom_real = 1.0 + scaled
    denom_imag = -scaled
    modulus = denom_real * denom_real + denom_imag * denom_imag
    pole_real = (numer_real * denom_real + scaled * denom_imag) / modulus
    pole_imag = (scaled * denom_real - numer_real * denom_imag) / modulus
    pole_norm = pole_real * pole_real + pole_imag * pole_imag
    zero_place = 1.0 if highpass else -1.0
    section_gain = ((1.0 + zero_place * pole_real) ** 2 + pole_imag * pole_imag) / 4.0
    linear = section_gain * (2.0 * pole_real - 2.0 * zero_place)
    constant = section_gain * (1.0 - pole_norm)
    shrink = 1.0 - math.sqrt(pole_norm)
    first_out = linear / shrink
    second = (constant + pole_real * linear) / (pole_imag * shrink)
    rotation = np.array([[pole_real, -pole_imag], [pole_imag, pole_real]])
    inject = np.array([shrink, 0.0])
    return (rotation, inject, np.array([first_out, second]), section_gain)


def filter_system():
    high_rotation, high_inject, high_out, high_gain = section(low_corner, True)
    low_rotation, low_inject, low_out, low_gain = section(high_corner, False)
    upper_rows = np.concatenate([high_rotation, np.zeros((2, 2))], axis=1)
    lower_rows = np.concatenate([np.outer(low_inject, high_out), low_rotation], axis=1)
    transition = np.concatenate([upper_rows, lower_rows], axis=0)
    driving = np.concatenate([high_inject, low_inject * high_gain])
    readout = np.concatenate([high_out * low_gain, low_out])
    direct = low_gain * high_gain
    return (transition, driving, readout, direct)


def spatial_taps(extent):
    positions = np.arange(-extent, extent + 1)
    window = 0.5 * (1.0 + np.cos(np.pi * positions / (extent + 1)))
    window = window / np.sum(window)
    return np.where(positions == 0, 1.0 - window, -window)


def chain(count, power, couple):
    powers = [np.eye(4)]
    for _ in range(count):
        powers.append(powers[-1] @ power)
    ahead = np.zeros((count, 4, count, 8))
    behind = np.zeros((count, 4, count, 8))
    for at in range(count):
        for other in range(at):
            ahead[at, :, other, :4] = powers[at - 1 - other]
    for at in range(count):
        for other in range(at + 1, count):
            gives = np.einsum("pq,qjr->pjr", couple, ahead[other])
            gives[:, other, 4:] += np.eye(4)
            behind[at] += np.einsum("pq,qjr->pjr", powers[other - 1 - at], gives)
    inner = np.concatenate([ahead, behind], axis=1)
    outer = np.zeros((count, 8, 8))
    for at in range(count):
        outer[at, :4, :4] = powers[at]
    for at in range(count):
        outer[at, 4:, 4:] = powers[count - 1 - at]
        for other in range(at + 1, count):
            outer[at, 4:, :4] += powers[other - 1 - at] @ couple @ outer[other, :4, :4]
    total = np.zeros((8, count, 8))
    for other in range(count):
        total[:4, other, :4] = powers[count - 1 - other]
        gives = np.einsum("pq,qjr->pjr", couple, ahead[other])
        gives[:, other, 4:] += np.eye(4)
        total[4:] += np.einsum("pq,qjr->pjr", powers[other], gives)
    pull = sum(powers[other] @ couple @ powers[other] for other in range(count))
    return inner, outer, total, powers[count], pull


def split(table):
    high = np.asarray(table, np.float32).astype(ml_dtypes.bfloat16)
    low = (np.asarray(table, np.float64) - high.astype(np.float64)).astype(np.float32)
    return high, low.astype(ml_dtypes.bfloat16)


def thrice(table):
    high, low = split(table)
    return np.concatenate([high, high, low], axis=0)


def beside(table):
    high, low = split(table)
    return np.concatenate([high, high, low], axis=1)


@functools.lru_cache(maxsize=None)
def filter_tables(blocks, devices):
    transition, driving, readout, direct = filter_system()
    powers = [np.eye(4)]
    for _ in range(BLOCK):
        powers.append(powers[-1] @ transition)
    response = np.array([direct] + [readout @ powers[lag] @ driving for lag in range(BLOCK - 1)])
    lag = np.arange(BLOCK)[:, None] - np.arange(BLOCK)[None, :]
    forward = np.where(lag >= 0, response[np.clip(lag, 0, BLOCK - 1)], 0.0)
    observe = np.stack([readout @ powers[at] for at in range(BLOCK)])
    reach = np.stack([powers[BLOCK - 1 - at] @ driving for at in range(BLOCK)], axis=1)
    both_ways = forward.T @ forward
    gives = np.concatenate([reach, reach[:, ::-1] @ forward], axis=0)
    takes = np.concatenate([forward.T @ observe, observe[::-1]], axis=1)
    couple = reach[:, ::-1] @ observe
    inner, outer, total, power, pull = chain(blocks, powers[BLOCK], couple)
    across = chain(devices, power, pull)[0]
    width = 8 * blocks
    first = thrice(np.tile(gives.T, (1, blocks)))
    main = thrice(both_ways)
    correct = thrice(np.tile(takes.T, (blocks, 1)))
    outside = thrice(np.concatenate([(takes @ outer[at]).T for at in range(blocks)], axis=1))
    gathers = across.reshape(devices, 8, devices, 4, 2).transpose(0, 3, 1, 2, 4)
    gathers = gathers.reshape(devices, 32, 2 * devices)
    return (
        first,
        beside(total.reshape(8, width)),
        main,
        thrice(inner.reshape(width, width).T),
        correct,
        np.stack([beside(gathers[at]) for at in range(devices)]),
        np.stack([beside(gathers[at][:, devices:]) for at in range(devices)]),
        outside,
    )


@functools.lru_cache(maxsize=None)
def space_tables(channels):
    taps = spatial_taps(RADIUS)

    def band(sources):
        lag = np.asarray(sources)[None, :] - np.arange(channels)[:, None] + RADIUS
        inside = (lag >= 0) & (lag <= 2 * RADIUS)
        return np.where(inside, taps[np.clip(lag, 0, 2 * RADIUS)], 0.0)

    own = band(np.arange(channels))
    edge = np.concatenate(
        [band(np.arange(-RADIUS, 0)), band(np.arange(channels, channels + RADIUS))], axis=1
    )
    parts = []
    for table in (edge, own):
        high, low = split(table)
        parts.append(np.concatenate([high, low, high], axis=1))
    states = np.zeros((channels, 3 * LANES))
    states[:, :channels] = own
    states[:, LANES : LANES + channels] = band(np.arange(-channels, 0))
    states[:, 2 * LANES : 2 * LANES + channels] = band(np.arange(channels, 2 * channels))
    return parts[0], parts[1], beside(states)


def halves(value):
    high = value.astype(jnp.bfloat16)
    return high, (value - high.astype(jnp.float32)).astype(jnp.bfloat16)


def product(left, right):
    return jnp.dot(left, right, preferred_element_type=jnp.float32)


def product_turned(left, right):
    turned = (((1,), (1,)), ((), ()))
    return lax.dot_general(left, right, turned, preferred_element_type=jnp.float32)


def tripled(value, axis):
    high, low = halves(value)
    return jnp.concatenate([high, low, high], axis=axis)


def kernel(
    devices,
    groups,
    x_hbm,
    mask_hbm,
    first_hbm,
    total_hbm,
    main_hbm,
    inner_hbm,
    correct_hbm,
    across_hbm,
    later_hbm,
    outside_hbm,
    edge_hbm,
    own_hbm,
    states_hbm,
    out,
    x,
    mask,
    first,
    total,
    main,
    inner,
    correct,
    across,
    later,
    outside,
    edge,
    own,
    states,
    halo,
    ends,
    entering,
    straight,
    packed_own,
    extra,
    parts,
    load_sem,
    x_sem,
    end_send,
    end_recv,
    near_send,
    near_recv,
    halo_send,
    halo_recv,
    straight_send,
    straight_recv,
    answer_sem,
    slow_sem,
):
    channels, samples = x.shape
    blocks = samples // BLOCK
    width = 8 * blocks
    row, column = lax.axis_index("tm"), lax.axis_index("chan")
    below, above = lax.rem(column + groups - 1, groups), lax.rem(column + 1, groups)
    up = (above, column < groups - 1, column > 0)
    down = (below, column > 0, column < groups - 1)
    half = devices // 2
    quarter_rows = half // 2
    chip, core = row // 2, row % 2
    early = row < half
    late = jnp.logical_not(early)
    slow = jnp.logical_and(row == 0, column == 0)
    quick = jnp.logical_not(slow)
    by_slow = jnp.logical_and(row == 0, column == 1)
    direct = jnp.logical_and(row < quarter_rows, quick)
    first_late, last = half // 2, half - 1
    relayed = half >= 8
    greeters = []
    for at in range(half):
        before = {k for k in range(min(at, first_late))}
        beside_it = {k for k in range(first_late, half) if at >= first_late and 0 < abs(k - at) <= 2}
        if relayed and at == last:
            before -= {first_late - 1}
        greeters.append(before | beside_it)
    order = sorted(range(1, devices), key=lambda step: abs(step - half))

    def is_one_of(value, places):
        return functools.reduce(jnp.logical_or, [value == place for place in places])

    def pick(values):
        return functools.reduce(
            jnp.add, [jnp.where(chip == at, value, 0) for at, value in enumerate(values)]
        )

    columns = ((0, column, column >= 0), (1, above, column < groups - 1), (2, below, column > 0))

    ends[...] = jnp.zeros_like(ends)
    straight[...] = jnp.zeros_like(straight)
    extra[...] = jnp.zeros_like(extra)

    quarter = samples // PIECES
    arrivals = []
    for piece in range(PIECES):
        span = pl.ds(piece * quarter, quarter)
        arrivals.append(pltpu.make_async_copy(x_hbm.at[:, span], x.at[:, span], x_sem.at[piece]))
    loads = []
    for index, (source, target) in enumerate(
        (
            (mask_hbm, mask),
            (first_hbm, first),
            (total_hbm, total),
            (main_hbm, main),
            (inner_hbm, inner),
            (correct_hbm, correct),
            (states_hbm, states),
            (across_hbm.at[row], across),
            (later_hbm.at[row], later),
            (own_hbm, own),
            (edge_hbm, edge),
            (outside_hbm, outside),
        )
    ):
        loads.append(pltpu.make_async_copy(source, target, load_sem.at[index]))
    for copy in (*arrivals, *loads[:3]):
        copy.start()

    barrier = pltpu.get_barrier_semaphore()

    def greet(there, to_row, to_column):
        @pl.when(there)
        def _():
            pl.semaphore_signal(
                barrier, inc=1, device_id=(to_row, to_column), device_id_type=MESH
            )

    for side, sends, gets in (up, down):
        greet(jnp.logical_and(sends, quick), row, side)
    greet(quick, chip * 2 + 1 - core, column)
    greet(jnp.logical_and(column == 0, chip > 0), 0, 0)
    for to in range(half):
        sources = sorted(k for k in greeters[to])
        if sources:

            @pl.when(jnp.logical_and(is_one_of(chip, sources), quick))
            def _():
                for at in range(2):
                    pl.semaphore_signal(
                        barrier, inc=1, device_id=(2 * to + at, column), device_id_type=MESH
                    )

    @pl.when(direct)
    def _():
        for place, side, there in columns[1:]:

            @pl.when(there)
            def _():
                for to in range(half, devices):
                    pl.semaphore_signal(
                        barrier, inc=1, device_id=(to, side), device_id_type=MESH
                    )

    for copy in loads[3:]:
        copy.start()

    @pl.when(slow)
    def _():
        pl.semaphore_wait(barrier, devices)
        pl.semaphore_signal(slow_sem, inc=1, device_id=(0, 1), device_id_type=MESH)
        for to in reversed(range(1, devices)):
            pl.semaphore_signal(slow_sem, inc=1, device_id=(to, 0), device_id_type=MESH)

    @pl.when(column == 0)
    def _():
        halo[pl.ds(0, RADIUS), :] = jnp.zeros((RADIUS, samples), jnp.float32)
        entering[1] = jnp.zeros((8, LANES), jnp.float32)

    @pl.when(column == groups - 1)
    def _():
        halo[pl.ds(RADIUS, RADIUS), :] = jnp.zeros((RADIUS, samples), jnp.float32)
        entering[2] = jnp.zeros((8, LANES), jnp.float32)

    loads[0].wait()
    here = lax.broadcasted_iota(jnp.int32, (channels, channels), 0)
    there = lax.broadcasted_iota(jnp.int32, (channels, channels), 1)
    live = jnp.where(here == there, mask[...].astype(jnp.float32), 0.0)
    live = jnp.sum(live, axis=1, keepdims=True)
    slot = lax.broadcasted_iota(jnp.int32, (channels, width), 1) // 8
    per = quarter // BLOCK
    given = jnp.zeros((channels, width), jnp.float32)
    for piece in range(PIECES):
        arrivals[piece].wait()
        at = [(piece * per + k) * BLOCK for k in range(per)]
        value = jnp.concatenate([x[:, k : k + BLOCK] * live for k in at], axis=0)
        triple = tripled(value, 1)
        size = per * channels
        parts[piece * size : (piece + 1) * size, :] = triple
        if piece == 0:
            loads[1].wait()
        answer = product(triple, first[...])
        for k in range(per):
            mine = answer[k * channels : (k + 1) * channels]
            given = given + jnp.where(slot == piece * per + k, mine, 0.0)
    given = tripled(given, 1)
    loads[2].wait()
    mine = product_turned(total[...], given)
    entering[0] = jnp.concatenate([mine, jnp.zeros((8, LANES - channels), jnp.float32)], axis=1)
    packed_own[...] = jnp.concatenate([mine[2 * k : 2 * k + 2] for k in range(4)], axis=1)

    def finish():
        for load in loads[3:6]:
            load.wait()
        high, low = halves(product(given, inner[...]))
        rows = []
        for k in range(blocks):
            k_high = jnp.where(slot == k, high, jnp.zeros_like(high))
            k_low = jnp.where(slot == k, low, jnp.zeros_like(low))
            rows.append(jnp.concatenate([k_high, k_low, k_high], axis=1))
        local = product(parts[...], main[...]) + product(
            jnp.concatenate(rows, axis=0), correct[...]
        )
        for k in range(blocks):
            x[:, k * BLOCK : (k + 1) * BLOCK] = local[k * channels : (k + 1) * channels]

    others = jnp.where(column > 0, 1, 0) + jnp.where(column < groups - 1, 1, 0)
    greeted = pick([1 + 2 * len(sources) for sources in greeters])
    greeted += others + jnp.where(early, 0, quarter_rows * others)
    missed = jnp.logical_and(column == 0, is_one_of(chip, [0, *range(1, half)]))
    missed = jnp.logical_or(missed, by_slow)
    missed = jnp.logical_or(missed, jnp.logical_and(column == 1, late))

    @pl.when(quick)
    def _():
        pl.semaphore_wait(barrier, greeted - jnp.where(missed, 1, 0))

    answers = []
    for to in range(first_late - 1):
        answers.append((first_late - 1, to))
    for to in range(first_late):
        answers.append((last - 1 if 2 * to < first_late else first_late + 1, to))
    if relayed:
        answers += [(last - 1, first_late), (first_late + 1, last)]
    for source in sorted({source for source, to in answers}):

        @pl.when(chip == source)
        def _():
            for to in [to for source_, to in answers if source_ == source]:

                @pl.when(jnp.logical_or(2 * to + core > 0, column > 0))
                def _():
                    pl.semaphore_signal(
                        answer_sem, inc=1, device_id=(2 * to + core, column), device_id_type=MESH
                    )

    near = []
    for way, (side, sends, gets) in enumerate((up, down)):
        copy = pltpu.make_async_remote_copy(
            src_ref=entering.at[0],
            dst_ref=entering.at[1 + way],
            send_sem=near_send.at[way],
            recv_sem=near_recv.at[way],
            device_id=(row, side),
            device_id_type=MESH,
        )
        now = sends if way == 0 else jnp.logical_and(sends, jnp.logical_not(by_slow))
        pl.when(now)(copy.start)
        near.append((copy, sends, gets))

    def goes(place, to, there):
        if to > 0 or place == 1:
            return there
        return jnp.logical_and(there, column > (0 if place == 0 else 1))

    def straight_copy(place, side, to, source):
        return pltpu.make_async_remote_copy(
            src_ref=packed_own,
            dst_ref=straight.at[place, source],
            send_sem=straight_send.at[place, to],
            recv_sem=straight_recv.at[place, source],
            device_id=(to, side),
            device_id_type=MESH,
        )

    @pl.when(late)
    def _():
        for to in range(quarter_rows):
            for place, side, there in columns:
                copy = straight_copy(place, side, to, row - half)
                pl.when(goes(place, to, there))(copy.start)

    finish()
    for load in loads[6:]:
        load.wait()

    length = samples // PIECES
    pieces = []
    for piece in range(PIECES):
        span = pl.ds(piece * length, length)
        pair = []
        for way, ((side, sends, gets), source, target) in enumerate(
            ((up, channels - RADIUS, 0), (down, 0, RADIUS))
        ):
            copy = pltpu.make_async_remote_copy(
                src_ref=x.at[pl.ds(source, RADIUS), span],
                dst_ref=halo.at[pl.ds(target, RADIUS), span],
                send_sem=halo_send.at[way, piece],
                recv_sem=halo_recv.at[way, piece],
                device_id=(row, side),
                device_id_type=MESH,
            )
            now = sends if way == 0 else jnp.logical_and(sends, jnp.logical_not(by_slow))
            pl.when(now)(copy.start)
            pair.append((copy, sends, gets))
        pieces.append(pair)

    @pl.when(by_slow)
    def _():
        pl.semaphore_wait(slow_sem, 1)
        near[1][0].start()
        for pair in pieces:
            pair[1][0].start()

    high, low = halves(x[...])
    out[...] = product(own[...], jnp.concatenate([high, high, low], axis=0))

    def receive(piece):
        for copy, sends, gets in pieces[piece]:
            pl.when(gets)(copy.wait_recv)
        begin, end = piece * length, (piece + 1) * length
        high, low = halves(halo[:, begin:end])
        out[:, begin:end] += product(edge[...], jnp.concatenate([high, high, low], axis=0))

    for copy, sends, gets in near:
        pl.when(gets)(copy.wait_recv)
    mine = product_turned(
        tripled(jnp.concatenate([entering[0], entering[1], entering[2]], axis=1), 1), states[...]
    )
    ends[row] = jnp.concatenate([mine[2 * k : 2 * k + 2] for k in range(4)], axis=1)

    def end_copy(to, slot_index):
        return pltpu.make_async_remote_copy(
            src_ref=ends.at[slot_index],
            dst_ref=ends.at[slot_index],
            send_sem=end_send.at[to],
            recv_sem=end_recv.at[slot_index],
            device_id=(to, column),
            device_id_type=MESH,
        )

    awaited = [len([to for source, to in answers if to == at]) for at in range(half)]

    @pl.when(jnp.logical_and(is_one_of(chip, [at for at in range(half) if awaited[at]]), quick))
    def _():
        pl.semaphore_wait(answer_sem, pick(awaited))

    def to_send(step):
        to = lax.rem(row + step, devices)
        to_slow = jnp.logical_and(to == 0, column == 0)
        return to, jnp.logical_and(
            jnp.logical_or(early, to >= quarter_rows), jnp.logical_not(to_slow)
        )

    def to_get(step):
        source = lax.rem(row + step, devices)
        return source, jnp.logical_or(jnp.logical_not(direct), source < half)

    for step in order:
        to, there = to_send(step)
        pl.when(there)(end_copy(to, row).start)

    in_column = jnp.logical_and(column == 0, row > 0)

    @pl.when(in_column)
    def _():
        pl.semaphore_wait(slow_sem, 1)
        end_copy(0, row).start()

    for piece in range(EARLY):
        receive(piece)

    for step in reversed(order):
        source, there = to_get(step)
        pl.when(there)(end_copy(row, source).wait_recv)

    def unpacked(value):
        folded = [
            pltpu.roll(value[8 * k : 8 * k + 8], LANES - 32 * k, axis=1) for k in range(1, 4)
        ]
        return value[0:8] + functools.reduce(jnp.add, folded)

    @pl.when(direct)
    def _():
        for source in range(half):
            for place, side, there in ((0, column, True), (1, below, up[2]), (2, above, down[2])):
                copy = straight_copy(place, side, 0, source)
                if place == 0:
                    copy.wait_recv()
                else:
                    pl.when(there)(copy.wait_recv)
        lane = lax.broadcasted_iota(jnp.int32, (8, LANES), 1)
        gathered = []
        for place in range(3):
            value = jnp.concatenate([straight[place, k] for k in range(half)], axis=0)
            value = unpacked(product(later[...], tripled(value, 0)))
            gathered.append(jnp.where(lane < channels, value, 0.0))
        extra[:, :channels] = product_turned(
            tripled(jnp.concatenate(gathered, axis=1), 1), states[...]
        )

    packed = jnp.concatenate([ends[k] for k in range(devices)], axis=0)
    mixed = product(across[...], tripled(packed, 0))
    taken = (unpacked(mixed) + extra[...])[:, :channels]

    for piece in range(EARLY, PIECES):
        receive(piece)

    out[...] += lax.dot_general(
        tripled(taken, 0),
        outside[...],
        (((0,), (0,)), ((), ())),
        preferred_element_type=jnp.float32,
    )

    for step in order:
        to, there = to_send(step)
        pl.when(there)(end_copy(to, row).wait_send)
    pl.when(in_column)(end_copy(0, row).wait_send)

    @pl.when(late)
    def _():
        for to in range(quarter_rows):
            for place, side, there in columns:
                copy = straight_copy(place, side, to, row - half)
                pl.when(goes(place, to, there))(copy.wait_send)

    for copy, sends, gets in near + [copy for pair in pieces for copy in pair]:
        pl.when(sends)(copy.wait_send)


def shards(devices, groups, strain, channel_mask):
    channels, samples = strain.shape
    tables = filter_tables(samples // BLOCK, devices) + space_tables(channels)
    tables = [jnp.asarray(table) for table in tables]
    f32 = jnp.float32
    held = [pltpu.VMEM(table.shape, table.dtype) for table in tables]
    for k in (5, 6):
        held[k] = pltpu.VMEM(tables[k].shape[1:], tables[k].dtype)
    return pl.pallas_call(
        functools.partial(kernel, devices, groups),
        out_shape=jax.ShapeDtypeStruct((channels, samples), f32),
        in_specs=[pl.BlockSpec(memory_space=pltpu.HBM)] * (2 + len(tables)),
        out_specs=pl.BlockSpec(memory_space=pltpu.VMEM),
        scratch_shapes=[
            pltpu.VMEM((channels, samples), f32),
            pltpu.VMEM((1, channels), jnp.int32),
            *held,
            pltpu.VMEM((2 * RADIUS, samples), f32),
            pltpu.VMEM((devices, 2, LANES), f32),
            pltpu.VMEM((3, 8, LANES), f32),
            pltpu.VMEM((3, devices // 2, 2, LANES), f32),
            pltpu.VMEM((2, LANES), f32),
            pltpu.VMEM((8, LANES), f32),
            pltpu.VMEM((channels * samples // BLOCK, 3 * BLOCK), jnp.bfloat16),
            pltpu.SemaphoreType.DMA((2 + len(tables),)),
            pltpu.SemaphoreType.DMA((PIECES,)),
            pltpu.SemaphoreType.DMA((devices,)),
            pltpu.SemaphoreType.DMA((devices,)),
            pltpu.SemaphoreType.DMA((2,)),
            pltpu.SemaphoreType.DMA((2,)),
            pltpu.SemaphoreType.DMA((2, PIECES)),
            pltpu.SemaphoreType.DMA((2, PIECES)),
            pltpu.SemaphoreType.DMA((3, devices // 2)),
            pltpu.SemaphoreType.DMA((3, devices // 2)),
            pltpu.SemaphoreType.REGULAR,
            pltpu.SemaphoreType.REGULAR,
        ],
        compiler_params=pltpu.CompilerParams(
            collective_id=0, has_side_effects=True, vmem_limit_bytes=40 * 1024 * 1024
        ),
        name="bandpass",
    )(
        *[
            pltpu.with_memory_space_constraint(value, pltpu.HBM)
            for value in (strain, channel_mask.reshape(1, channels), *tables)
        ]
    )


def solution(mesh):
    placed = (P("chan", "tm"), P("chan"))
    sizes = dict(zip(mesh.axis_names, mesh.devices.shape))
    return jax.shard_map(
        functools.partial(shards, sizes["tm"], sizes["chan"]),
        mesh=mesh,
        in_specs=placed,
        out_specs=P("chan", "tm"),
        check_vma=False,
    )
```

```python
import functools
import math

import jax
import jax.numpy as jnp
import ml_dtypes
import numpy as np
from jax import lax
from jax.experimental import pallas as pl
from jax.experimental.pallas import tpu as pltpu
from jax.sharding import PartitionSpec as P

RADIUS = 16
BLOCK = 256
LANES = 128
PIECES = 4
EARLY = 3

low_corner = 0.015
high_corner = 100.0
sample_rate = 500.0
MESH = pl.DeviceIdType.MESH


def section(corner, highpass):
    warped = 2.0 * sample_rate * math.tan(math.pi * corner / sample_rate)
    scaled = warped / (2.0 * sample_rate * math.sqrt(2.0))
    numer_real = 1.0 - scaled
    denom_real = 1.0 + scaled
    denom_imag = -scaled
    modulus = denom_real * denom_real + denom_imag * denom_imag
    pole_real = (numer_real * denom_real + scaled * denom_imag) / modulus
    pole_imag = (scaled * denom_real - numer_real * denom_imag) / modulus
    pole_norm = pole_real * pole_real + pole_imag * pole_imag
    zero_place = 1.0 if highpass else -1.0
    section_gain = ((1.0 + zero_place * pole_real) ** 2 + pole_imag * pole_imag) / 4.0
    linear = section_gain * (2.0 * pole_real - 2.0 * zero_place)
    constant = section_gain * (1.0 - pole_norm)
    shrink = 1.0 - math.sqrt(pole_norm)
    first_out = linear / shrink
    second = (constant + pole_real * linear) / (pole_imag * shrink)
    rotation = np.array([[pole_real, -pole_imag], [pole_imag, pole_real]])
    inject = np.array([shrink, 0.0])
    return (rotation, inject, np.array([first_out, second]), section_gain)


def filter_system():
    high_rotation, high_inject, high_out, high_gain = section(low_corner, True)
    low_rotation, low_inject, low_out, low_gain = section(high_corner, False)
    upper_rows = np.concatenate([high_rotation, np.zeros((2, 2))], axis=1)
    lower_rows = np.concatenate([np.outer(low_inject, high_out), low_rotation], axis=1)
    transition = np.concatenate([upper_rows, lower_rows], axis=0)
    driving = np.concatenate([high_inject, low_inject * high_gain])
    readout = np.concatenate([high_out * low_gain, low_out])
    direct = low_gain * high_gain
    return (transition, driving, readout, direct)


def spatial_taps(extent):
    positions = np.arange(-extent, extent + 1)
    window = 0.5 * (1.0 + np.cos(np.pi * positions / (extent + 1)))
    window = window / np.sum(window)
    return np.where(positions == 0, 1.0 - window, -window)


def chain(count, power, couple):
    powers = [np.eye(4)]
    for _ in range(count):
        powers.append(powers[-1] @ power)
    ahead = np.zeros((count, 4, count, 8))
    behind = np.zeros((count, 4, count, 8))
    for at in range(count):
        for other in range(at):
            ahead[at, :, other, :4] = powers[at - 1 - other]
    for at in range(count):
        for other in range(at + 1, count):
            gives = np.einsum("pq,qjr->pjr", couple, ahead[other])
            gives[:, other, 4:] += np.eye(4)
            behind[at] += np.einsum("pq,qjr->pjr", powers[other - 1 - at], gives)
    inner = np.concatenate([ahead, behind], axis=1)
    outer = np.zeros((count, 8, 8))
    for at in range(count):
        outer[at, :4, :4] = powers[at]
    for at in range(count):
        outer[at, 4:, 4:] = powers[count - 1 - at]
        for other in range(at + 1, count):
            outer[at, 4:, :4] += powers[other - 1 - at] @ couple @ outer[other, :4, :4]
    total = np.zeros((8, count, 8))
    for other in range(count):
        total[:4, other, :4] = powers[count - 1 - other]
        gives = np.einsum("pq,qjr->pjr", couple, ahead[other])
        gives[:, other, 4:] += np.eye(4)
        total[4:] += np.einsum("pq,qjr->pjr", powers[other], gives)
    pull = sum(powers[other] @ couple @ powers[other] for other in range(count))
    return inner, outer, total, powers[count], pull


def split(table):
    high = np.asarray(table, np.float32).astype(ml_dtypes.bfloat16)
    low = (np.asarray(table, np.float64) - high.astype(np.float64)).astype(np.float32)
    return high, low.astype(ml_dtypes.bfloat16)


def thrice(table):
    high, low = split(table)
    return np.concatenate([high, high, low], axis=0)


def beside(table):
    high, low = split(table)
    return np.concatenate([high, high, low], axis=1)


@functools.lru_cache(maxsize=None)
def filter_tables(blocks, devices):
    transition, driving, readout, direct = filter_system()
    powers = [np.eye(4)]
    for _ in range(BLOCK):
        powers.append(powers[-1] @ transition)
    response = np.array([direct] + [readout @ powers[lag] @ driving for lag in range(BLOCK - 1)])
    lag = np.arange(BLOCK)[:, None] - np.arange(BLOCK)[None, :]
    forward = np.where(lag >= 0, response[np.clip(lag, 0, BLOCK - 1)], 0.0)
    observe = np.stack([readout @ powers[at] for at in range(BLOCK)])
    reach = np.stack([powers[BLOCK - 1 - at] @ driving for at in range(BLOCK)], axis=1)
    both_ways = forward.T @ forward
    gives = np.concatenate([reach, reach[:, ::-1] @ forward], axis=0)
    takes = np.concatenate([forward.T @ observe, observe[::-1]], axis=1)
    couple = reach[:, ::-1] @ observe
    inner, outer, total, power, pull = chain(blocks, powers[BLOCK], couple)
    across = chain(devices, power, pull)[0]
    width = 8 * blocks
    first = thrice(np.tile(gives.T, (1, blocks)))
    main = thrice(both_ways)
    correct = thrice(np.tile(takes.T, (blocks, 1)))
    outside = thrice(np.concatenate([(takes @ outer[at]).T for at in range(blocks)], axis=1))
    gathers = across.reshape(devices, 8, devices, 4, 2).transpose(0, 3, 1, 2, 4)
    gathers = gathers.reshape(devices, 32, 2 * devices)
    return (
        first,
        beside(total.reshape(8, width)),
        main,
        thrice(inner.reshape(width, width).T),
        correct,
        np.stack([beside(gathers[at]) for at in range(devices)]),
        np.stack([beside(gathers[at][:, devices:]) for at in range(devices)]),
        outside,
    )


@functools.lru_cache(maxsize=None)
def space_tables(channels):
    taps = spatial_taps(RADIUS)

    def band(sources):
        lag = np.asarray(sources)[None, :] - np.arange(channels)[:, None] + RADIUS
        inside = (lag >= 0) & (lag <= 2 * RADIUS)
        return np.where(inside, taps[np.clip(lag, 0, 2 * RADIUS)], 0.0)

    own = band(np.arange(channels))
    edge = np.concatenate(
        [band(np.arange(-RADIUS, 0)), band(np.arange(channels, channels + RADIUS))], axis=1
    )
    parts = []
    for table in (edge, own):
        high, low = split(table)
        parts.append(np.concatenate([high, low, high], axis=1))
    states = np.zeros((channels, 3 * LANES))
    states[:, :channels] = own
    states[:, LANES : LANES + channels] = band(np.arange(-channels, 0))
    states[:, 2 * LANES : 2 * LANES + channels] = band(np.arange(channels, 2 * channels))
    return parts[0], parts[1], beside(states)


def halves(value):
    high = value.astype(jnp.bfloat16)
    return high, (value - high.astype(jnp.float32)).astype(jnp.bfloat16)


def product(left, right):
    return jnp.dot(left, right, preferred_element_type=jnp.float32)


def product_turned(left, right):
    turned = (((1,), (1,)), ((), ()))
    return lax.dot_general(left, right, turned, preferred_element_type=jnp.float32)


def tripled(value, axis):
    high, low = halves(value)
    return jnp.concatenate([high, low, high], axis=axis)


def kernel(
    devices,
    groups,
    x_hbm,
    mask_hbm,
    first_hbm,
    total_hbm,
    main_hbm,
    inner_hbm,
    correct_hbm,
    across_hbm,
    later_hbm,
    outside_hbm,
    edge_hbm,
    own_hbm,
    states_hbm,
    out,
    x,
    mask,
    first,
    total,
    main,
    inner,
    correct,
    across,
    later,
    outside,
    edge,
    own,
    states,
    halo,
    ends,
    entering,
    straight,
    packed_own,
    extra,
    parts,
    load_sem,
    x_sem,
    end_send,
    end_recv,
    near_send,
    near_recv,
    halo_send,
    halo_recv,
    straight_send,
    straight_recv,
    answer_sem,
    slow_sem,
):
    channels, samples = x.shape
    blocks = samples // BLOCK
    width = 8 * blocks
    row, column = lax.axis_index("tm"), lax.axis_index("chan")
    below, above = lax.rem(column + groups - 1, groups), lax.rem(column + 1, groups)
    up = (above, column < groups - 1, column > 0)
    down = (below, column > 0, column < groups - 1)
    half = devices // 2
    quarter_rows = half // 2
    chip, core = row // 2, row % 2
    early = row < half
    late = jnp.logical_not(early)
    slow = jnp.logical_and(row == 0, column == 0)
    quick = jnp.logical_not(slow)
    by_slow = jnp.logical_and(row == 0, column == 1)
    direct = jnp.logical_and(row < quarter_rows, quick)
    first_late, last = half // 2, half - 1
    relayed = half >= 8
    greeters = []
    for at in range(half):
        before = {k for k in range(min(at, first_late))}
        beside_it = {k for k in range(first_late, half) if at >= first_late and 0 < abs(k - at) <= 2}
        if relayed and at == last:
            before -= {first_late - 1}
        greeters.append(before | beside_it)
    order = sorted(range(1, devices), key=lambda step: abs(step - half))

    def is_one_of(value, places):
        return functools.reduce(jnp.logical_or, [value == place for place in places])

    def pick(values):
        return functools.reduce(
            jnp.add, [jnp.where(chip == at, value, 0) for at, value in enumerate(values)]
        )

    columns = ((0, column, column >= 0), (1, above, column < groups - 1), (2, below, column > 0))

    ends[...] = jnp.zeros_like(ends)
    straight[...] = jnp.zeros_like(straight)
    extra[...] = jnp.zeros_like(extra)

    barrier = pltpu.get_barrier_semaphore()

    def greet(there, to_row, to_column):
        @pl.when(there)
        def _():
            pl.semaphore_signal(
                barrier, inc=1, device_id=(to_row, to_column), device_id_type=MESH
            )

    for side, sends, gets in (up, down):
        greet(jnp.logical_and(sends, quick), row, side)

    quarter = samples // PIECES
    arrivals = []
    for piece in range(PIECES):
        span = pl.ds(piece * quarter, quarter)
        arrivals.append(pltpu.make_async_copy(x_hbm.at[:, span], x.at[:, span], x_sem.at[piece]))
    loads = []
    for index, (source, target) in enumerate(
        (
            (mask_hbm, mask),
            (first_hbm, first),
            (total_hbm, total),
            (main_hbm, main),
            (inner_hbm, inner),
            (correct_hbm, correct),
            (states_hbm, states),
            (across_hbm.at[row], across),
            (later_hbm.at[row], later),
            (own_hbm, own),
            (edge_hbm, edge),
            (outside_hbm, outside),
        )
    ):
        loads.append(pltpu.make_async_copy(source, target, load_sem.at[index]))
    for copy in (*arrivals, *loads[:3]):
        copy.start()

    greet(quick, chip * 2 + 1 - core, column)
    greet(jnp.logical_and(column == 0, chip > 0), 0, 0)
    for to in range(half):
        sources = sorted(k for k in greeters[to])
        if sources:

            @pl.when(jnp.logical_and(is_one_of(chip, sources), quick))
            def _():
                for at in range(2):
                    pl.semaphore_signal(
                        barrier, inc=1, device_id=(2 * to + at, column), device_id_type=MESH
                    )

    @pl.when(direct)
    def _():
        for place, side, there in columns[1:]:

            @pl.when(there)
            def _():
                for to in range(half, devices):
                    pl.semaphore_signal(
                        barrier, inc=1, device_id=(to, side), device_id_type=MESH
                    )

    for copy in loads[3:]:
        copy.start()

    @pl.when(slow)
    def _():
        pl.semaphore_wait(barrier, devices)
        pl.semaphore_signal(slow_sem, inc=1, device_id=(0, 1), device_id_type=MESH)
        for to in reversed(range(1, devices)):
            pl.semaphore_signal(slow_sem, inc=1, device_id=(to, 0), device_id_type=MESH)

    @pl.when(column == 0)
    def _():
        halo[pl.ds(0, RADIUS), :] = jnp.zeros((RADIUS, samples), jnp.float32)
        entering[1] = jnp.zeros((8, LANES), jnp.float32)

    @pl.when(column == groups - 1)
    def _():
        halo[pl.ds(RADIUS, RADIUS), :] = jnp.zeros((RADIUS, samples), jnp.float32)
        entering[2] = jnp.zeros((8, LANES), jnp.float32)

    loads[0].wait()
    here = lax.broadcasted_iota(jnp.int32, (channels, channels), 0)
    there = lax.broadcasted_iota(jnp.int32, (channels, channels), 1)
    live = jnp.where(here == there, mask[...].astype(jnp.float32), 0.0)
    live = jnp.sum(live, axis=1, keepdims=True)
    slot = lax.broadcasted_iota(jnp.int32, (channels, width), 1) // 8
    per = quarter // BLOCK
    given = jnp.zeros((channels, width), jnp.float32)
    for piece in range(PIECES):
        arrivals[piece].wait()
        at = [(piece * per + k) * BLOCK for k in range(per)]
        value = jnp.concatenate([x[:, k : k + BLOCK] * live for k in at], axis=0)
        triple = tripled(value, 1)
        size = per * channels
        parts[piece * size : (piece + 1) * size, :] = triple
        if piece == 0:
            loads[1].wait()
        answer = product(triple, first[...])
        for k in range(per):
            mine = answer[k * channels : (k + 1) * channels]
            given = given + jnp.where(slot == piece * per + k, mine, 0.0)
    given = tripled(given, 1)
    loads[2].wait()
    mine = product_turned(total[...], given)
    entering[0] = jnp.concatenate([mine, jnp.zeros((8, LANES - channels), jnp.float32)], axis=1)
    packed_own[...] = jnp.concatenate([mine[2 * k : 2 * k + 2] for k in range(4)], axis=1)

    others = jnp.where(column > 0, 1, 0) + jnp.where(column < groups - 1, 1, 0)
    greeted = pick([1 + 2 * len(sources) for sources in greeters])
    greeted += others + jnp.where(early, 0, quarter_rows * others)
    missed = jnp.logical_and(column == 0, is_one_of(chip, [0, *range(1, half)]))
    missed = jnp.logical_or(missed, by_slow)
    missed = jnp.logical_or(missed, jnp.logical_and(column == 1, late))

    @pl.when(quick)
    def _():
        pl.semaphore_wait(barrier, greeted - jnp.where(missed, 1, 0))

    answers = []
    for to in range(first_late - 1):
        answers.append((first_late - 1, to))
    for to in range(first_late):
        answers.append((last - 1 if 2 * to < first_late else first_late + 1, to))
    if relayed:
        answers += [(last - 1, first_late), (first_late + 1, last)]
    for source in sorted({source for source, to in answers}):

        @pl.when(chip == source)
        def _():
            for to in [to for source_, to in answers if source_ == source]:

                @pl.when(jnp.logical_or(2 * to + core > 0, column > 0))
                def _():
                    pl.semaphore_signal(
                        answer_sem, inc=1, device_id=(2 * to + core, column), device_id_type=MESH
                    )

    near = []
    for way, (side, sends, gets) in enumerate((up, down)):
        copy = pltpu.make_async_remote_copy(
            src_ref=entering.at[0],
            dst_ref=entering.at[1 + way],
            send_sem=near_send.at[way],
            recv_sem=near_recv.at[way],
            device_id=(row, side),
            device_id_type=MESH,
        )
        now = sends if way == 0 else jnp.logical_and(sends, jnp.logical_not(by_slow))
        pl.when(now)(copy.start)
        near.append((copy, sends, gets))

    def goes(place, to, there):
        if to > 0 or place == 1:
            return there
        return jnp.logical_and(there, column > (0 if place == 0 else 1))

    def straight_copy(place, side, to, source):
        return pltpu.make_async_remote_copy(
            src_ref=packed_own,
            dst_ref=straight.at[place, source],
            send_sem=straight_send.at[place, to],
            recv_sem=straight_recv.at[place, source],
            device_id=(to, side),
            device_id_type=MESH,
        )

    @pl.when(late)
    def _():
        for to in range(quarter_rows):
            for place, side, there in columns:
                copy = straight_copy(place, side, to, row - half)
                pl.when(goes(place, to, there))(copy.start)

    for load in loads[3:6]:
        load.wait()
    high, low = halves(product(given, inner[...]))
    length = samples // PIECES
    pieces = []
    for piece in range(PIECES):
        rows = []
        for k in range(piece * per, (piece + 1) * per):
            k_high = jnp.where(slot == k, high, jnp.zeros_like(high))
            k_low = jnp.where(slot == k, low, jnp.zeros_like(low))
            rows.append(jnp.concatenate([k_high, k_low, k_high], axis=1))
        size = per * channels
        local = product(parts[piece * size : (piece + 1) * size, :], main[...]) + product(
            jnp.concatenate(rows, axis=0), correct[...]
        )
        for k in range(per):
            at = piece * length + k * BLOCK
            x[:, at : at + BLOCK] = local[k * channels : (k + 1) * channels]
        span = pl.ds(piece * length, length)
        pair = []
        for way, ((side, sends, gets), source, target) in enumerate(
            ((up, channels - RADIUS, 0), (down, 0, RADIUS))
        ):
            copy = pltpu.make_async_remote_copy(
                src_ref=x.at[pl.ds(source, RADIUS), span],
                dst_ref=halo.at[pl.ds(target, RADIUS), span],
                send_sem=halo_send.at[way, piece],
                recv_sem=halo_recv.at[way, piece],
                device_id=(row, side),
                device_id_type=MESH,
            )
            now = sends if way == 0 else jnp.logical_and(sends, jnp.logical_not(by_slow))
            pl.when(now)(copy.start)
            pair.append((copy, sends, gets))
        pieces.append(pair)
    for load in loads[6:]:
        load.wait()

    @pl.when(by_slow)
    def _():
        pl.semaphore_wait(slow_sem, 1)
        near[1][0].start()
        for pair in pieces:
            pair[1][0].start()

    high, low = halves(x[...])
    out[...] = product(own[...], jnp.concatenate([high, high, low], axis=0))

    def receive(piece):
        for copy, sends, gets in pieces[piece]:
            pl.when(gets)(copy.wait_recv)
        begin, end = piece * length, (piece + 1) * length
        high, low = halves(halo[:, begin:end])
        out[:, begin:end] += product(edge[...], jnp.concatenate([high, high, low], axis=0))

    for copy, sends, gets in near:
        pl.when(gets)(copy.wait_recv)
    mine = product_turned(
        tripled(jnp.concatenate([entering[0], entering[1], entering[2]], axis=1), 1), states[...]
    )
    ends[row] = jnp.concatenate([mine[2 * k : 2 * k + 2] for k in range(4)], axis=1)

    def end_copy(to, slot_index):
        return pltpu.make_async_remote_copy(
            src_ref=ends.at[slot_index],
            dst_ref=ends.at[slot_index],
            send_sem=end_send.at[to],
            recv_sem=end_recv.at[slot_index],
            device_id=(to, column),
            device_id_type=MESH,
        )

    awaited = [len([to for source, to in answers if to == at]) for at in range(half)]

    @pl.when(jnp.logical_and(is_one_of(chip, [at for at in range(half) if awaited[at]]), quick))
    def _():
        pl.semaphore_wait(answer_sem, pick(awaited))

    def to_send(step):
        to = lax.rem(row + step, devices)
        to_slow = jnp.logical_and(to == 0, column == 0)
        return to, jnp.logical_and(
            jnp.logical_or(early, to >= quarter_rows), jnp.logical_not(to_slow)
        )

    def to_get(step):
        source = lax.rem(row + step, devices)
        return source, jnp.logical_or(jnp.logical_not(direct), source < half)

    for step in order:
        to, there = to_send(step)
        pl.when(there)(end_copy(to, row).start)

    in_column = jnp.logical_and(column == 0, row > 0)

    @pl.when(in_column)
    def _():
        pl.semaphore_wait(slow_sem, 1)
        end_copy(0, row).start()

    for piece in range(EARLY):
        receive(piece)

    for step in order:
        to, there = to_send(step)
        pl.when(there)(end_copy(to, row).wait_send)
    pl.when(in_column)(end_copy(0, row).wait_send)

    @pl.when(late)
    def _():
        for to in range(quarter_rows):
            for place, side, there in columns:
                copy = straight_copy(place, side, to, row - half)
                pl.when(goes(place, to, there))(copy.wait_send)

    for copy, sends, gets in near + [copy for pair in pieces[:-1] for copy in pair]:
        pl.when(sends)(copy.wait_send)

    for step in reversed(order):
        source, there = to_get(step)
        pl.when(there)(end_copy(row, source).wait_recv)

    def unpacked(value):
        folded = [
            pltpu.roll(value[8 * k : 8 * k + 8], LANES - 32 * k, axis=1) for k in range(1, 4)
        ]
        return value[0:8] + functools.reduce(jnp.add, folded)

    @pl.when(direct)
    def _():
        for source in range(half):
            for place, side, there in ((0, column, True), (1, below, up[2]), (2, above, down[2])):
                copy = straight_copy(place, side, 0, source)
                if place == 0:
                    copy.wait_recv()
                else:
                    pl.when(there)(copy.wait_recv)
        lane = lax.broadcasted_iota(jnp.int32, (8, LANES), 1)
        gathered = []
        for place in range(3):
            value = jnp.concatenate([straight[place, k] for k in range(half)], axis=0)
            value = unpacked(product(later[...], tripled(value, 0)))
            gathered.append(jnp.where(lane < channels, value, 0.0))
        extra[:, :channels] = product_turned(
            tripled(jnp.concatenate(gathered, axis=1), 1), states[...]
        )

    packed = jnp.concatenate([ends[k] for k in range(devices)], axis=0)
    mixed = product(across[...], tripled(packed, 0))
    taken = (unpacked(mixed) + extra[...])[:, :channels]

    for piece in range(EARLY, PIECES):
        receive(piece)

    out[...] += lax.dot_general(
        tripled(taken, 0),
        outside[...],
        (((0,), (0,)), ((), ())),
        preferred_element_type=jnp.float32,
    )

    for copy, sends, gets in pieces[-1]:
        pl.when(sends)(copy.wait_send)


def shards(devices, groups, strain, channel_mask):
    channels, samples = strain.shape
    tables = filter_tables(samples // BLOCK, devices) + space_tables(channels)
    tables = [jnp.asarray(table) for table in tables]
    f32 = jnp.float32
    held = [pltpu.VMEM(table.shape, table.dtype) for table in tables]
    for k in (5, 6):
        held[k] = pltpu.VMEM(tables[k].shape[1:], tables[k].dtype)
    return pl.pallas_call(
        functools.partial(kernel, devices, groups),
        out_shape=jax.ShapeDtypeStruct((channels, samples), f32),
        in_specs=[pl.BlockSpec(memory_space=pltpu.HBM)] * (2 + len(tables)),
        out_specs=pl.BlockSpec(memory_space=pltpu.VMEM),
        scratch_shapes=[
            pltpu.VMEM((channels, samples), f32),
            pltpu.VMEM((1, channels), jnp.int32),
            *held,
            pltpu.VMEM((2 * RADIUS, samples), f32),
            pltpu.VMEM((devices, 2, LANES), f32),
            pltpu.VMEM((3, 8, LANES), f32),
            pltpu.VMEM((3, devices // 2, 2, LANES), f32),
            pltpu.VMEM((2, LANES), f32),
            pltpu.VMEM((8, LANES), f32),
            pltpu.VMEM((channels * samples // BLOCK, 3 * BLOCK), jnp.bfloat16),
            pltpu.SemaphoreType.DMA((2 + len(tables),)),
            pltpu.SemaphoreType.DMA((PIECES,)),
            pltpu.SemaphoreType.DMA((devices,)),
            pltpu.SemaphoreType.DMA((devices,)),
            pltpu.SemaphoreType.DMA((2,)),
            pltpu.SemaphoreType.DMA((2,)),
            pltpu.SemaphoreType.DMA((2, PIECES)),
            pltpu.SemaphoreType.DMA((2, PIECES)),
            pltpu.SemaphoreType.DMA((3, devices // 2)),
            pltpu.SemaphoreType.DMA((3, devices // 2)),
            pltpu.SemaphoreType.REGULAR,
            pltpu.SemaphoreType.REGULAR,
        ],
        compiler_params=pltpu.CompilerParams(
            collective_id=0, has_side_effects=True, vmem_limit_bytes=40 * 1024 * 1024
        ),
        name="bandpass",
    )(
        *[
            pltpu.with_memory_space_constraint(value, pltpu.HBM)
            for value in (strain, channel_mask.reshape(1, channels), *tables)
        ]
    )


def solution(mesh):
    placed = (P("chan", "tm"), P("chan"))
    sizes = dict(zip(mesh.axis_names, mesh.devices.shape))
    return jax.shard_map(
        functools.partial(shards, sizes["tm"], sizes["chan"]),
        mesh=mesh,
        in_specs=placed,
        out_specs=P("chan", "tm"),
        check_vma=False,
    )
```

```python
import functools
import math

import jax
import jax.numpy as jnp
import ml_dtypes
import numpy as np
from jax import lax
from jax.experimental import pallas as pl
from jax.experimental.pallas import tpu as pltpu
from jax.sharding import PartitionSpec as P

RADIUS = 16
BLOCK = 256
LANES = 128
PIECES = 2
EARLY = 1

low_corner = 0.015
high_corner = 100.0
sample_rate = 500.0
MESH = pl.DeviceIdType.MESH


def section(corner, highpass):
    warped = 2.0 * sample_rate * math.tan(math.pi * corner / sample_rate)
    scaled = warped / (2.0 * sample_rate * math.sqrt(2.0))
    numer_real = 1.0 - scaled
    denom_real = 1.0 + scaled
    denom_imag = -scaled
    modulus = denom_real * denom_real + denom_imag * denom_imag
    pole_real = (numer_real * denom_real + scaled * denom_imag) / modulus
    pole_imag = (scaled * denom_real - numer_real * denom_imag) / modulus
    pole_norm = pole_real * pole_real + pole_imag * pole_imag
    zero_place = 1.0 if highpass else -1.0
    section_gain = ((1.0 + zero_place * pole_real) ** 2 + pole_imag * pole_imag) / 4.0
    linear = section_gain * (2.0 * pole_real - 2.0 * zero_place)
    constant = section_gain * (1.0 - pole_norm)
    shrink = 1.0 - math.sqrt(pole_norm)
    first_out = linear / shrink
    second = (constant + pole_real * linear) / (pole_imag * shrink)
    rotation = np.array([[pole_real, -pole_imag], [pole_imag, pole_real]])
    inject = np.array([shrink, 0.0])
    return (rotation, inject, np.array([first_out, second]), section_gain)


def filter_system():
    high_rotation, high_inject, high_out, high_gain = section(low_corner, True)
    low_rotation, low_inject, low_out, low_gain = section(high_corner, False)
    upper_rows = np.concatenate([high_rotation, np.zeros((2, 2))], axis=1)
    lower_rows = np.concatenate([np.outer(low_inject, high_out), low_rotation], axis=1)
    transition = np.concatenate([upper_rows, lower_rows], axis=0)
    driving = np.concatenate([high_inject, low_inject * high_gain])
    readout = np.concatenate([high_out * low_gain, low_out])
    direct = low_gain * high_gain
    return (transition, driving, readout, direct)


def spatial_taps(extent):
    positions = np.arange(-extent, extent + 1)
    window = 0.5 * (1.0 + np.cos(np.pi * positions / (extent + 1)))
    window = window / np.sum(window)
    return np.where(positions == 0, 1.0 - window, -window)


def chain(count, power, couple):
    powers = [np.eye(4)]
    for _ in range(count):
        powers.append(powers[-1] @ power)
    ahead = np.zeros((count, 4, count, 8))
    behind = np.zeros((count, 4, count, 8))
    for at in range(count):
        for other in range(at):
            ahead[at, :, other, :4] = powers[at - 1 - other]
    for at in range(count):
        for other in range(at + 1, count):
            gives = np.einsum("pq,qjr->pjr", couple, ahead[other])
            gives[:, other, 4:] += np.eye(4)
            behind[at] += np.einsum("pq,qjr->pjr", powers[other - 1 - at], gives)
    inner = np.concatenate([ahead, behind], axis=1)
    outer = np.zeros((count, 8, 8))
    for at in range(count):
        outer[at, :4, :4] = powers[at]
    for at in range(count):
        outer[at, 4:, 4:] = powers[count - 1 - at]
        for other in range(at + 1, count):
            outer[at, 4:, :4] += powers[other - 1 - at] @ couple @ outer[other, :4, :4]
    total = np.zeros((8, count, 8))
    for other in range(count):
        total[:4, other, :4] = powers[count - 1 - other]
        gives = np.einsum("pq,qjr->pjr", couple, ahead[other])
        gives[:, other, 4:] += np.eye(4)
        total[4:] += np.einsum("pq,qjr->pjr", powers[other], gives)
    pull = sum(powers[other] @ couple @ powers[other] for other in range(count))
    return inner, outer, total, powers[count], pull


def split(table):
    high = np.asarray(table, np.float32).astype(ml_dtypes.bfloat16)
    low = (np.asarray(table, np.float64) - high.astype(np.float64)).astype(np.float32)
    return high, low.astype(ml_dtypes.bfloat16)


def thrice(table):
    high, low = split(table)
    return np.concatenate([high, high, low], axis=0)


def beside(table):
    high, low = split(table)
    return np.concatenate([high, high, low], axis=1)


@functools.lru_cache(maxsize=None)
def filter_tables(blocks, devices):
    transition, driving, readout, direct = filter_system()
    powers = [np.eye(4)]
    for _ in range(BLOCK):
        powers.append(powers[-1] @ transition)
    response = np.array([direct] + [readout @ powers[lag] @ driving for lag in range(BLOCK - 1)])
    lag = np.arange(BLOCK)[:, None] - np.arange(BLOCK)[None, :]
    forward = np.where(lag >= 0, response[np.clip(lag, 0, BLOCK - 1)], 0.0)
    observe = np.stack([readout @ powers[at] for at in range(BLOCK)])
    reach = np.stack([powers[BLOCK - 1 - at] @ driving for at in range(BLOCK)], axis=1)
    both_ways = forward.T @ forward
    gives = np.concatenate([reach, reach[:, ::-1] @ forward], axis=0)
    takes = np.concatenate([forward.T @ observe, observe[::-1]], axis=1)
    couple = reach[:, ::-1] @ observe
    inner, outer, total, power, pull = chain(blocks, powers[BLOCK], couple)
    across = chain(devices, power, pull)[0]
    width = 8 * blocks
    first = thrice(np.tile(gives.T, (1, blocks)))
    main = thrice(both_ways)
    correct = thrice(np.tile(takes.T, (blocks, 1)))
    outside = thrice(np.concatenate([(takes @ outer[at]).T for at in range(blocks)], axis=1))
    gathers = across.reshape(devices, 8, devices, 4, 2).transpose(0, 3, 1, 2, 4)
    gathers = gathers.reshape(devices, 32, 2 * devices)
    return (
        first,
        beside(total.reshape(8, width)),
        main,
        thrice(inner.reshape(width, width).T),
        correct,
        np.stack([beside(gathers[at]) for at in range(devices)]),
        np.stack([beside(gathers[at][:, devices:]) for at in range(devices)]),
        outside,
    )


@functools.lru_cache(maxsize=None)
def space_tables(channels):
    taps = spatial_taps(RADIUS)

    def band(sources):
        lag = np.asarray(sources)[None, :] - np.arange(channels)[:, None] + RADIUS
        inside = (lag >= 0) & (lag <= 2 * RADIUS)
        return np.where(inside, taps[np.clip(lag, 0, 2 * RADIUS)], 0.0)

    own = band(np.arange(channels))
    edge = np.concatenate(
        [band(np.arange(-RADIUS, 0)), band(np.arange(channels, channels + RADIUS))], axis=1
    )
    parts = []
    for table in (edge, own):
        high, low = split(table)
        parts.append(np.concatenate([high, low, high], axis=1))
    states = np.zeros((channels, 3 * LANES))
    states[:, :channels] = own
    states[:, LANES : LANES + channels] = band(np.arange(-channels, 0))
    states[:, 2 * LANES : 2 * LANES + channels] = band(np.arange(channels, 2 * channels))
    return parts[0], parts[1], beside(states)


def halves(value):
    high = value.astype(jnp.bfloat16)
    return high, (value - high.astype(jnp.float32)).astype(jnp.bfloat16)


def product(left, right):
    return jnp.dot(left, right, preferred_element_type=jnp.float32)


def product_turned(left, right):
    turned = (((1,), (1,)), ((), ()))
    return lax.dot_general(left, right, turned, preferred_element_type=jnp.float32)


def tripled(value, axis):
    high, low = halves(value)
    return jnp.concatenate([high, low, high], axis=axis)


def kernel(
    devices,
    groups,
    x_hbm,
    mask_hbm,
    first_hbm,
    total_hbm,
    main_hbm,
    inner_hbm,
    correct_hbm,
    across_hbm,
    later_hbm,
    outside_hbm,
    edge_hbm,
    own_hbm,
    states_hbm,
    out,
    x,
    mask,
    first,
    total,
    main,
    inner,
    correct,
    across,
    later,
    outside,
    edge,
    own,
    states,
    halo,
    ends,
    entering,
    straight,
    packed_own,
    extra,
    parts,
    load_sem,
    x_sem,
    end_send,
    end_recv,
    near_send,
    near_recv,
    halo_send,
    halo_recv,
    straight_send,
    straight_recv,
    answer_sem,
    slow_sem,
):
    channels, samples = x.shape
    blocks = samples // BLOCK
    width = 8 * blocks
    row, column = lax.axis_index("tm"), lax.axis_index("chan")
    below, above = lax.rem(column + groups - 1, groups), lax.rem(column + 1, groups)
    up = (above, column < groups - 1, column > 0)
    down = (below, column > 0, column < groups - 1)
    half = devices // 2
    quarter_rows = half // 2
    chip, core = row // 2, row % 2
    early = row < half
    late = jnp.logical_not(early)
    slow = jnp.logical_and(row == 0, column == 0)
    quick = jnp.logical_not(slow)
    by_slow = jnp.logical_and(row == 0, column == 1)
    direct = jnp.logical_and(row < quarter_rows, quick)
    first_late, last = half // 2, half - 1
    relayed = half >= 8
    greeters = []
    for at in range(half):
        before = {k for k in range(min(at, first_late))}
        beside_it = {k for k in range(first_late, half) if at >= first_late and 0 < abs(k - at) <= 2}
        if relayed and at == last:
            before -= {first_late - 1}
        greeters.append(before | beside_it)
    order = sorted(range(1, devices), key=lambda step: abs(step - half))

    def is_one_of(value, places):
        return functools.reduce(jnp.logical_or, [value == place for place in places])

    def pick(values):
        return functools.reduce(
            jnp.add, [jnp.where(chip == at, value, 0) for at, value in enumerate(values)]
        )

    columns = ((0, column, column >= 0), (1, above, column < groups - 1), (2, below, column > 0))

    ends[...] = jnp.zeros_like(ends)
    straight[...] = jnp.zeros_like(straight)
    extra[...] = jnp.zeros_like(extra)

    barrier = pltpu.get_barrier_semaphore()

    def greet(there, to_row, to_column):
        @pl.when(there)
        def _():
            pl.semaphore_signal(
                barrier, inc=1, device_id=(to_row, to_column), device_id_type=MESH
            )

    for side, sends, gets in (up, down):
        greet(jnp.logical_and(sends, quick), row, side)

    quarter = samples // PIECES
    arrivals = []
    for piece in range(PIECES):
        span = pl.ds(piece * quarter, quarter)
        arrivals.append(pltpu.make_async_copy(x_hbm.at[:, span], x.at[:, span], x_sem.at[piece]))
    loads = []
    for index, (source, target) in enumerate(
        (
            (mask_hbm, mask),
            (first_hbm, first),
            (total_hbm, total),
            (main_hbm, main),
            (inner_hbm, inner),
            (correct_hbm, correct),
            (states_hbm, states),
            (across_hbm.at[row], across),
            (later_hbm.at[row], later),
            (own_hbm, own),
            (edge_hbm, edge),
            (outside_hbm, outside),
        )
    ):
        loads.append(pltpu.make_async_copy(source, target, load_sem.at[index]))
    for copy in (*arrivals, *loads[:3]):
        copy.start()

    greet(quick, chip * 2 + 1 - core, column)
    greet(jnp.logical_and(column == 0, chip > 0), 0, 0)
    for to in range(half):
        sources = sorted(k for k in greeters[to])
        if sources:

            @pl.when(jnp.logical_and(is_one_of(chip, sources), quick))
            def _():
                for at in range(2):
                    pl.semaphore_signal(
                        barrier, inc=1, device_id=(2 * to + at, column), device_id_type=MESH
                    )

    @pl.when(direct)
    def _():
        for place, side, there in columns[1:]:

            @pl.when(there)
            def _():
                for to in range(half, devices):
                    pl.semaphore_signal(
                        barrier, inc=1, device_id=(to, side), device_id_type=MESH
                    )

    for copy in loads[3:]:
        copy.start()

    @pl.when(slow)
    def _():
        pl.semaphore_wait(barrier, devices)
        pl.semaphore_signal(slow_sem, inc=1, device_id=(0, 1), device_id_type=MESH)
        for to in reversed(range(1, devices)):
            pl.semaphore_signal(slow_sem, inc=1, device_id=(to, 0), device_id_type=MESH)

    @pl.when(column == 0)
    def _():
        halo[pl.ds(0, RADIUS), :] = jnp.zeros((RADIUS, samples), jnp.float32)
        entering[1] = jnp.zeros((8, LANES), jnp.float32)

    @pl.when(column == groups - 1)
    def _():
        halo[pl.ds(RADIUS, RADIUS), :] = jnp.zeros((RADIUS, samples), jnp.float32)
        entering[2] = jnp.zeros((8, LANES), jnp.float32)

    loads[0].wait()
    here = lax.broadcasted_iota(jnp.int32, (channels, channels), 0)
    there = lax.broadcasted_iota(jnp.int32, (channels, channels), 1)
    live = jnp.where(here == there, mask[...].astype(jnp.float32), 0.0)
    live = jnp.sum(live, axis=1, keepdims=True)
    slot = lax.broadcasted_iota(jnp.int32, (channels, width), 1) // 8
    per = quarter // BLOCK
    given = jnp.zeros((channels, width), jnp.float32)
    for piece in range(PIECES):
        arrivals[piece].wait()
        at = [(piece * per + k) * BLOCK for k in range(per)]
        value = jnp.concatenate([x[:, k : k + BLOCK] * live for k in at], axis=0)
        triple = tripled(value, 1)
        size = per * channels
        parts[piece * size : (piece + 1) * size, :] = triple
        if piece == 0:
            loads[1].wait()
        answer = product(triple, first[...])
        for k in range(per):
            mine = answer[k * channels : (k + 1) * channels]
            given = given + jnp.where(slot == piece * per + k, mine, 0.0)
    given = tripled(given, 1)
    loads[2].wait()
    mine = product_turned(total[...], given)
    entering[0] = jnp.concatenate([mine, jnp.zeros((8, LANES - channels), jnp.float32)], axis=1)
    packed_own[...] = jnp.concatenate([mine[2 * k : 2 * k + 2] for k in range(4)], axis=1)

    others = jnp.where(column > 0, 1, 0) + jnp.where(column < groups - 1, 1, 0)
    greeted = pick([1 + 2 * len(sources) for sources in greeters])
    greeted += others + jnp.where(early, 0, quarter_rows * others)
    missed = jnp.logical_and(column == 0, is_one_of(chip, [0, *range(1, half)]))
    missed = jnp.logical_or(missed, by_slow)
    missed = jnp.logical_or(missed, jnp.logical_and(column == 1, late))

    @pl.when(quick)
    def _():
        pl.semaphore_wait(barrier, greeted - jnp.where(missed, 1, 0))

    answers = []
    for to in range(first_late - 1):
        answers.append((first_late - 1, to))
    for to in range(first_late):
        answers.append((last - 1 if 2 * to < first_late else first_late + 1, to))
    if relayed:
        answers += [(last - 1, first_late), (first_late + 1, last)]
    for source in sorted({source for source, to in answers}):

        @pl.when(chip == source)
        def _():
            for to in [to for source_, to in answers if source_ == source]:

                @pl.when(jnp.logical_or(2 * to + core > 0, column > 0))
                def _():
                    pl.semaphore_signal(
                        answer_sem, inc=1, device_id=(2 * to + core, column), device_id_type=MESH
                    )

    near = []
    for way, (side, sends, gets) in enumerate((up, down)):
        copy = pltpu.make_async_remote_copy(
            src_ref=entering.at[0],
            dst_ref=entering.at[1 + way],
            send_sem=near_send.at[way],
            recv_sem=near_recv.at[way],
            device_id=(row, side),
            device_id_type=MESH,
        )
        now = sends if way == 0 else jnp.logical_and(sends, jnp.logical_not(by_slow))
        pl.when(now)(copy.start)
        near.append((copy, sends, gets))

    def goes(place, to, there):
        if to > 0 or place == 1:
            return there
        return jnp.logical_and(there, column > (0 if place == 0 else 1))

    def straight_copy(place, side, to, source):
        return pltpu.make_async_remote_copy(
            src_ref=packed_own,
            dst_ref=straight.at[place, source],
            send_sem=straight_send.at[place, to],
            recv_sem=straight_recv.at[place, source],
            device_id=(to, side),
            device_id_type=MESH,
        )

    @pl.when(late)
    def _():
        for to in range(quarter_rows):
            for place, side, there in columns:
                copy = straight_copy(place, side, to, row - half)
                pl.when(goes(place, to, there))(copy.start)

    for load in loads[3:6]:
        load.wait()
    high, low = halves(product(given, inner[...]))
    length = samples // PIECES
    pieces = []
    for piece in range(PIECES):
        rows = []
        for k in range(piece * per, (piece + 1) * per):
            k_high = jnp.where(slot == k, high, jnp.zeros_like(high))
            k_low = jnp.where(slot == k, low, jnp.zeros_like(low))
            rows.append(jnp.concatenate([k_high, k_low, k_high], axis=1))
        size = per * channels
        local = product(parts[piece * size : (piece + 1) * size, :], main[...]) + product(
            jnp.concatenate(rows, axis=0), correct[...]
        )
        for k in range(per):
            at = piece * length + k * BLOCK
            x[:, at : at + BLOCK] = local[k * channels : (k + 1) * channels]
        span = pl.ds(piece * length, length)
        pair = []
        for way, ((side, sends, gets), source, target) in enumerate(
            ((up, channels - RADIUS, 0), (down, 0, RADIUS))
        ):
            copy = pltpu.make_async_remote_copy(
                src_ref=x.at[pl.ds(source, RADIUS), span],
                dst_ref=halo.at[pl.ds(target, RADIUS), span],
                send_sem=halo_send.at[way, piece],
                recv_sem=halo_recv.at[way, piece],
                device_id=(row, side),
                device_id_type=MESH,
            )
            now = sends if way == 0 else jnp.logical_and(sends, jnp.logical_not(by_slow))
            pl.when(now)(copy.start)
            pair.append((copy, sends, gets))
        pieces.append(pair)
    for load in loads[6:]:
        load.wait()

    @pl.when(by_slow)
    def _():
        pl.semaphore_wait(slow_sem, 1)
        near[1][0].start()
        for pair in pieces:
            pair[1][0].start()

    high, low = halves(x[...])
    out[...] = product(own[...], jnp.concatenate([high, high, low], axis=0))

    def receive(piece):
        for copy, sends, gets in pieces[piece]:
            pl.when(gets)(copy.wait_recv)
        begin, end = piece * length, (piece + 1) * length
        high, low = halves(halo[:, begin:end])
        out[:, begin:end] += product(edge[...], jnp.concatenate([high, high, low], axis=0))

    for copy, sends, gets in near:
        pl.when(gets)(copy.wait_recv)
    mine = product_turned(
        tripled(jnp.concatenate([entering[0], entering[1], entering[2]], axis=1), 1), states[...]
    )
    ends[row] = jnp.concatenate([mine[2 * k : 2 * k + 2] for k in range(4)], axis=1)

    def end_copy(to, slot_index):
        return pltpu.make_async_remote_copy(
            src_ref=ends.at[slot_index],
            dst_ref=ends.at[slot_index],
            send_sem=end_send.at[to],
            recv_sem=end_recv.at[slot_index],
            device_id=(to, column),
            device_id_type=MESH,
        )

    awaited = [len([to for source, to in answers if to == at]) for at in range(half)]

    @pl.when(jnp.logical_and(is_one_of(chip, [at for at in range(half) if awaited[at]]), quick))
    def _():
        pl.semaphore_wait(answer_sem, pick(awaited))

    def to_send(step):
        to = lax.rem(row + step, devices)
        to_slow = jnp.logical_and(to == 0, column == 0)
        return to, jnp.logical_and(
            jnp.logical_or(early, to >= quarter_rows), jnp.logical_not(to_slow)
        )

    def to_get(step):
        source = lax.rem(row + step, devices)
        return source, jnp.logical_or(jnp.logical_not(direct), source < half)

    for step in order:
        to, there = to_send(step)
        pl.when(there)(end_copy(to, row).start)

    in_column = jnp.logical_and(column == 0, row > 0)

    @pl.when(in_column)
    def _():
        pl.semaphore_wait(slow_sem, 1)
        end_copy(0, row).start()

    for piece in range(EARLY):
        receive(piece)

    for step in order:
        to, there = to_send(step)
        pl.when(there)(end_copy(to, row).wait_send)
    pl.when(in_column)(end_copy(0, row).wait_send)

    @pl.when(late)
    def _():
        for to in range(quarter_rows):
            for place, side, there in columns:
                copy = straight_copy(place, side, to, row - half)
                pl.when(goes(place, to, there))(copy.wait_send)

    for copy, sends, gets in near + [copy for pair in pieces[:-1] for copy in pair]:
        pl.when(sends)(copy.wait_send)

    for step in reversed(order):
        source, there = to_get(step)
        pl.when(there)(end_copy(row, source).wait_recv)

    def unpacked(value):
        folded = [
            pltpu.roll(value[8 * k : 8 * k + 8], LANES - 32 * k, axis=1) for k in range(1, 4)
        ]
        return value[0:8] + functools.reduce(jnp.add, folded)

    @pl.when(direct)
    def _():
        for source in range(half):
            for place, side, there in ((0, column, True), (1, below, up[2]), (2, above, down[2])):
                copy = straight_copy(place, side, 0, source)
                if place == 0:
                    copy.wait_recv()
                else:
                    pl.when(there)(copy.wait_recv)
        lane = lax.broadcasted_iota(jnp.int32, (8, LANES), 1)
        gathered = []
        for place in range(3):
            value = jnp.concatenate([straight[place, k] for k in range(half)], axis=0)
            value = unpacked(product(later[...], tripled(value, 0)))
            gathered.append(jnp.where(lane < channels, value, 0.0))
        extra[:, :channels] = product_turned(
            tripled(jnp.concatenate(gathered, axis=1), 1), states[...]
        )

    packed = jnp.concatenate([ends[k] for k in range(devices)], axis=0)
    mixed = product(across[...], tripled(packed, 0))
    taken = (unpacked(mixed) + extra[...])[:, :channels]

    for piece in range(EARLY, PIECES):
        receive(piece)

    out[...] += lax.dot_general(
        tripled(taken, 0),
        outside[...],
        (((0,), (0,)), ((), ())),
        preferred_element_type=jnp.float32,
    )

    for copy, sends, gets in pieces[-1]:
        pl.when(sends)(copy.wait_send)


def shards(devices, groups, strain, channel_mask):
    channels, samples = strain.shape
    tables = filter_tables(samples // BLOCK, devices) + space_tables(channels)
    tables = [jnp.asarray(table) for table in tables]
    f32 = jnp.float32
    held = [pltpu.VMEM(table.shape, table.dtype) for table in tables]
    for k in (5, 6):
        held[k] = pltpu.VMEM(tables[k].shape[1:], tables[k].dtype)
    return pl.pallas_call(
        functools.partial(kernel, devices, groups),
        out_shape=jax.ShapeDtypeStruct((channels, samples), f32),
        in_specs=[pl.BlockSpec(memory_space=pltpu.HBM)] * (2 + len(tables)),
        out_specs=pl.BlockSpec(memory_space=pltpu.VMEM),
        scratch_shapes=[
            pltpu.VMEM((channels, samples), f32),
            pltpu.VMEM((1, channels), jnp.int32),
            *held,
            pltpu.VMEM((2 * RADIUS, samples), f32),
            pltpu.VMEM((devices, 2, LANES), f32),
            pltpu.VMEM((3, 8, LANES), f32),
            pltpu.VMEM((3, devices // 2, 2, LANES), f32),
            pltpu.VMEM((2, LANES), f32),
            pltpu.VMEM((8, LANES), f32),
            pltpu.VMEM((channels * samples // BLOCK, 3 * BLOCK), jnp.bfloat16),
            pltpu.SemaphoreType.DMA((2 + len(tables),)),
            pltpu.SemaphoreType.DMA((PIECES,)),
            pltpu.SemaphoreType.DMA((devices,)),
            pltpu.SemaphoreType.DMA((devices,)),
            pltpu.SemaphoreType.DMA((2,)),
            pltpu.SemaphoreType.DMA((2,)),
            pltpu.SemaphoreType.DMA((2, PIECES)),
            pltpu.SemaphoreType.DMA((2, PIECES)),
            pltpu.SemaphoreType.DMA((3, devices // 2)),
            pltpu.SemaphoreType.DMA((3, devices // 2)),
            pltpu.SemaphoreType.REGULAR,
            pltpu.SemaphoreType.REGULAR,
        ],
        compiler_params=pltpu.CompilerParams(
            collective_id=0, has_side_effects=True, vmem_limit_bytes=40 * 1024 * 1024
        ),
        name="bandpass",
    )(
        *[
            pltpu.with_memory_space_constraint(value, pltpu.HBM)
            for value in (strain, channel_mask.reshape(1, channels), *tables)
        ]
    )


def solution(mesh):
    placed = (P("chan", "tm"), P("chan"))
    sizes = dict(zip(mesh.axis_names, mesh.devices.shape))
    return jax.shard_map(
        functools.partial(shards, sizes["tm"], sizes["chan"]),
        mesh=mesh,
        in_specs=placed,
        out_specs=P("chan", "tm"),
        check_vma=False,
    )
```

```python
import functools
import math

import jax
import jax.numpy as jnp
import ml_dtypes
import numpy as np
from jax import lax
from jax.experimental import pallas as pl
from jax.experimental.pallas import tpu as pltpu
from jax.sharding import PartitionSpec as P

RADIUS = 16
BLOCK = 256
LANES = 128
PIECES = 2
LOADS = 4
EARLY = 1

low_corner = 0.015
high_corner = 100.0
sample_rate = 500.0
MESH = pl.DeviceIdType.MESH


def section(corner, highpass):
    warped = 2.0 * sample_rate * math.tan(math.pi * corner / sample_rate)
    scaled = warped / (2.0 * sample_rate * math.sqrt(2.0))
    numer_real = 1.0 - scaled
    denom_real = 1.0 + scaled
    denom_imag = -scaled
    modulus = denom_real * denom_real + denom_imag * denom_imag
    pole_real = (numer_real * denom_real + scaled * denom_imag) / modulus
    pole_imag = (scaled * denom_real - numer_real * denom_imag) / modulus
    pole_norm = pole_real * pole_real + pole_imag * pole_imag
    zero_place = 1.0 if highpass else -1.0
    section_gain = ((1.0 + zero_place * pole_real) ** 2 + pole_imag * pole_imag) / 4.0
    linear = section_gain * (2.0 * pole_real - 2.0 * zero_place)
    constant = section_gain * (1.0 - pole_norm)
    shrink = 1.0 - math.sqrt(pole_norm)
    first_out = linear / shrink
    second = (constant + pole_real * linear) / (pole_imag * shrink)
    rotation = np.array([[pole_real, -pole_imag], [pole_imag, pole_real]])
    inject = np.array([shrink, 0.0])
    return (rotation, inject, np.array([first_out, second]), section_gain)


def filter_system():
    high_rotation, high_inject, high_out, high_gain = section(low_corner, True)
    low_rotation, low_inject, low_out, low_gain = section(high_corner, False)
    upper_rows = np.concatenate([high_rotation, np.zeros((2, 2))], axis=1)
    lower_rows = np.concatenate([np.outer(low_inject, high_out), low_rotation], axis=1)
    transition = np.concatenate([upper_rows, lower_rows], axis=0)
    driving = np.concatenate([high_inject, low_inject * high_gain])
    readout = np.concatenate([high_out * low_gain, low_out])
    direct = low_gain * high_gain
    return (transition, driving, readout, direct)


def spatial_taps(extent):
    positions = np.arange(-extent, extent + 1)
    window = 0.5 * (1.0 + np.cos(np.pi * positions / (extent + 1)))
    window = window / np.sum(window)
    return np.where(positions == 0, 1.0 - window, -window)


def chain(count, power, couple):
    powers = [np.eye(4)]
    for _ in range(count):
        powers.append(powers[-1] @ power)
    ahead = np.zeros((count, 4, count, 8))
    behind = np.zeros((count, 4, count, 8))
    for at in range(count):
        for other in range(at):
            ahead[at, :, other, :4] = powers[at - 1 - other]
    for at in range(count):
        for other in range(at + 1, count):
            gives = np.einsum("pq,qjr->pjr", couple, ahead[other])
            gives[:, other, 4:] += np.eye(4)
            behind[at] += np.einsum("pq,qjr->pjr", powers[other - 1 - at], gives)
    inner = np.concatenate([ahead, behind], axis=1)
    outer = np.zeros((count, 8, 8))
    for at in range(count):
        outer[at, :4, :4] = powers[at]
    for at in range(count):
        outer[at, 4:, 4:] = powers[count - 1 - at]
        for other in range(at + 1, count):
            outer[at, 4:, :4] += powers[other - 1 - at] @ couple @ outer[other, :4, :4]
    total = np.zeros((8, count, 8))
    for other in range(count):
        total[:4, other, :4] = powers[count - 1 - other]
        gives = np.einsum("pq,qjr->pjr", couple, ahead[other])
        gives[:, other, 4:] += np.eye(4)
        total[4:] += np.einsum("pq,qjr->pjr", powers[other], gives)
    pull = sum(powers[other] @ couple @ powers[other] for other in range(count))
    return inner, outer, total, powers[count], pull


def split(table):
    high = np.asarray(table, np.float32).astype(ml_dtypes.bfloat16)
    low = (np.asarray(table, np.float64) - high.astype(np.float64)).astype(np.float32)
    return high, low.astype(ml_dtypes.bfloat16)


def thrice(table):
    high, low = split(table)
    return np.concatenate([high, high, low], axis=0)


def beside(table):
    high, low = split(table)
    return np.concatenate([high, high, low], axis=1)


@functools.lru_cache(maxsize=None)
def filter_tables(blocks, devices):
    transition, driving, readout, direct = filter_system()
    powers = [np.eye(4)]
    for _ in range(BLOCK):
        powers.append(powers[-1] @ transition)
    response = np.array([direct] + [readout @ powers[lag] @ driving for lag in range(BLOCK - 1)])
    lag = np.arange(BLOCK)[:, None] - np.arange(BLOCK)[None, :]
    forward = np.where(lag >= 0, response[np.clip(lag, 0, BLOCK - 1)], 0.0)
    observe = np.stack([readout @ powers[at] for at in range(BLOCK)])
    reach = np.stack([powers[BLOCK - 1 - at] @ driving for at in range(BLOCK)], axis=1)
    both_ways = forward.T @ forward
    gives = np.concatenate([reach, reach[:, ::-1] @ forward], axis=0)
    takes = np.concatenate([forward.T @ observe, observe[::-1]], axis=1)
    couple = reach[:, ::-1] @ observe
    inner, outer, total, power, pull = chain(blocks, powers[BLOCK], couple)
    across = chain(devices, power, pull)[0]
    width = 8 * blocks
    first = thrice(np.tile(gives.T, (1, blocks)))
    main = thrice(both_ways)
    correct = thrice(np.tile(takes.T, (blocks, 1)))
    outside = thrice(np.concatenate([(takes @ outer[at]).T for at in range(blocks)], axis=1))
    gathers = across.reshape(devices, 8, devices, 4, 2).transpose(0, 3, 1, 2, 4)
    gathers = gathers.reshape(devices, 32, 2 * devices)
    return (
        first,
        beside(total.reshape(8, width)),
        main,
        thrice(inner.reshape(width, width).T),
        correct,
        np.stack([beside(gathers[at]) for at in range(devices)]),
        np.stack([beside(gathers[at][:, devices:]) for at in range(devices)]),
        outside,
    )


@functools.lru_cache(maxsize=None)
def space_tables(channels):
    taps = spatial_taps(RADIUS)

    def band(sources):
        lag = np.asarray(sources)[None, :] - np.arange(channels)[:, None] + RADIUS
        inside = (lag >= 0) & (lag <= 2 * RADIUS)
        return np.where(inside, taps[np.clip(lag, 0, 2 * RADIUS)], 0.0)

    own = band(np.arange(channels))
    edge = np.concatenate(
        [band(np.arange(-RADIUS, 0)), band(np.arange(channels, channels + RADIUS))], axis=1
    )
    parts = []
    for table in (edge, own):
        high, low = split(table)
        parts.append(np.concatenate([high, low, high], axis=1))
    states = np.zeros((channels, 3 * LANES))
    states[:, :channels] = own
    states[:, LANES : LANES + channels] = band(np.arange(-channels, 0))
    states[:, 2 * LANES : 2 * LANES + channels] = band(np.arange(channels, 2 * channels))
    return parts[0], parts[1], beside(states)


def halves(value):
    high = value.astype(jnp.bfloat16)
    return high, (value - high.astype(jnp.float32)).astype(jnp.bfloat16)


def product(left, right):
    return jnp.dot(left, right, preferred_element_type=jnp.float32)


def product_turned(left, right):
    turned = (((1,), (1,)), ((), ()))
    return lax.dot_general(left, right, turned, preferred_element_type=jnp.float32)


def tripled(value, axis):
    high, low = halves(value)
    return jnp.concatenate([high, low, high], axis=axis)


def kernel(
    devices,
    groups,
    x_hbm,
    mask_hbm,
    first_hbm,
    total_hbm,
    main_hbm,
    inner_hbm,
    correct_hbm,
    across_hbm,
    later_hbm,
    outside_hbm,
    edge_hbm,
    own_hbm,
    states_hbm,
    out,
    x,
    mask,
    first,
    total,
    main,
    inner,
    correct,
    across,
    later,
    outside,
    edge,
    own,
    states,
    halo,
    ends,
    entering,
    straight,
    packed_own,
    extra,
    parts,
    load_sem,
    x_sem,
    end_send,
    end_recv,
    near_send,
    near_recv,
    halo_send,
    halo_recv,
    straight_send,
    straight_recv,
    answer_sem,
    slow_sem,
):
    channels, samples = x.shape
    blocks = samples // BLOCK
    width = 8 * blocks
    row, column = lax.axis_index("tm"), lax.axis_index("chan")
    below, above = lax.rem(column + groups - 1, groups), lax.rem(column + 1, groups)
    up = (above, column < groups - 1, column > 0)
    down = (below, column > 0, column < groups - 1)
    half = devices // 2
    quarter_rows = half // 2
    chip, core = row // 2, row % 2
    early = row < half
    late = jnp.logical_not(early)
    slow = jnp.logical_and(row == 0, column == 0)
    quick = jnp.logical_not(slow)
    by_slow = jnp.logical_and(row == 0, column == 1)
    direct = jnp.logical_and(row < quarter_rows, quick)
    first_late, last = half // 2, half - 1
    relayed = half >= 8
    greeters = []
    for at in range(half):
        before = {k for k in range(min(at, first_late))}
        beside_it = {k for k in range(first_late, half) if at >= first_late and 0 < abs(k - at) <= 2}
        if relayed and at == last:
            before -= {first_late - 1}
        greeters.append(before | beside_it)
    order = sorted(range(1, devices), key=lambda step: abs(step - half))

    def is_one_of(value, places):
        return functools.reduce(jnp.logical_or, [value == place for place in places])

    def pick(values):
        return functools.reduce(
            jnp.add, [jnp.where(chip == at, value, 0) for at, value in enumerate(values)]
        )

    columns = ((0, column, column >= 0), (1, above, column < groups - 1), (2, below, column > 0))

    ends[...] = jnp.zeros_like(ends)
    straight[...] = jnp.zeros_like(straight)
    extra[...] = jnp.zeros_like(extra)

    barrier = pltpu.get_barrier_semaphore()

    def greet(there, to_row, to_column):
        @pl.when(there)
        def _():
            pl.semaphore_signal(
                barrier, inc=1, device_id=(to_row, to_column), device_id_type=MESH
            )

    for side, sends, gets in (up, down):
        greet(jnp.logical_and(sends, quick), row, side)

    quarter = samples // LOADS
    arrivals = []
    for piece in range(LOADS):
        span = pl.ds(piece * quarter, quarter)
        arrivals.append(pltpu.make_async_copy(x_hbm.at[:, span], x.at[:, span], x_sem.at[piece]))
    loads = []
    for index, (source, target) in enumerate(
        (
            (mask_hbm, mask),
            (first_hbm, first),
            (total_hbm, total),
            (main_hbm, main),
            (inner_hbm, inner),
            (correct_hbm, correct),
            (states_hbm, states),
            (across_hbm.at[row], across),
            (later_hbm.at[row], later),
            (own_hbm, own),
            (edge_hbm, edge),
            (outside_hbm, outside),
        )
    ):
        loads.append(pltpu.make_async_copy(source, target, load_sem.at[index]))
    for copy in (*arrivals, *loads[:3]):
        copy.start()

    greet(quick, chip * 2 + 1 - core, column)
    greet(jnp.logical_and(column == 0, chip > 0), 0, 0)
    for to in range(half):
        sources = sorted(k for k in greeters[to])
        if sources:

            @pl.when(jnp.logical_and(is_one_of(chip, sources), quick))
            def _():
                for at in range(2):
                    pl.semaphore_signal(
                        barrier, inc=1, device_id=(2 * to + at, column), device_id_type=MESH
                    )

    @pl.when(direct)
    def _():
        for place, side, there in columns[1:]:

            @pl.when(there)
            def _():
                for to in range(half, devices):
                    pl.semaphore_signal(
                        barrier, inc=1, device_id=(to, side), device_id_type=MESH
                    )

    for copy in loads[3:]:
        copy.start()

    @pl.when(slow)
    def _():
        pl.semaphore_wait(barrier, devices)
        pl.semaphore_signal(slow_sem, inc=1, device_id=(0, 1), device_id_type=MESH)
        for to in reversed(range(1, devices)):
            pl.semaphore_signal(slow_sem, inc=1, device_id=(to, 0), device_id_type=MESH)

    @pl.when(column == 0)
    def _():
        halo[pl.ds(0, RADIUS), :] = jnp.zeros((RADIUS, samples), jnp.float32)
        entering[1] = jnp.zeros((8, LANES), jnp.float32)

    @pl.when(column == groups - 1)
    def _():
        halo[pl.ds(RADIUS, RADIUS), :] = jnp.zeros((RADIUS, samples), jnp.float32)
        entering[2] = jnp.zeros((8, LANES), jnp.float32)

    loads[0].wait()
    here = lax.broadcasted_iota(jnp.int32, (channels, channels), 0)
    there = lax.broadcasted_iota(jnp.int32, (channels, channels), 1)
    live = jnp.where(here == there, mask[...].astype(jnp.float32), 0.0)
    live = jnp.sum(live, axis=1, keepdims=True)
    slot = lax.broadcasted_iota(jnp.int32, (channels, width), 1) // 8
    per = quarter // BLOCK
    given = jnp.zeros((channels, width), jnp.float32)
    for piece in range(LOADS):
        arrivals[piece].wait()
        at = [(piece * per + k) * BLOCK for k in range(per)]
        value = jnp.concatenate([x[:, k : k + BLOCK] * live for k in at], axis=0)
        triple = tripled(value, 1)
        size = per * channels
        parts[piece * size : (piece + 1) * size, :] = triple
        if piece == 0:
            loads[1].wait()
        answer = product(triple, first[...])
        for k in range(per):
            mine = answer[k * channels : (k + 1) * channels]
            given = given + jnp.where(slot == piece * per + k, mine, 0.0)
    given = tripled(given, 1)
    loads[2].wait()
    mine = product_turned(total[...], given)
    entering[0] = jnp.concatenate([mine, jnp.zeros((8, LANES - channels), jnp.float32)], axis=1)
    packed_own[...] = jnp.concatenate([mine[2 * k : 2 * k + 2] for k in range(4)], axis=1)

    others = jnp.where(column > 0, 1, 0) + jnp.where(column < groups - 1, 1, 0)
    greeted = pick([1 + 2 * len(sources) for sources in greeters])
    greeted += others + jnp.where(early, 0, quarter_rows * others)
    missed = jnp.logical_and(column == 0, is_one_of(chip, [0, *range(1, half)]))
    missed = jnp.logical_or(missed, by_slow)
    missed = jnp.logical_or(missed, jnp.logical_and(column == 1, late))

    @pl.when(quick)
    def _():
        pl.semaphore_wait(barrier, greeted - jnp.where(missed, 1, 0))

    answers = []
    for to in range(first_late - 1):
        answers.append((first_late - 1, to))
    for to in range(first_late):
        answers.append((last - 1 if 2 * to < first_late else first_late + 1, to))
    if relayed:
        answers += [(last - 1, first_late), (first_late + 1, last)]
    for source in sorted({source for source, to in answers}):

        @pl.when(chip == source)
        def _():
            for to in [to for source_, to in answers if source_ == source]:

                @pl.when(jnp.logical_or(2 * to + core > 0, column > 0))
                def _():
                    pl.semaphore_signal(
                        answer_sem, inc=1, device_id=(2 * to + core, column), device_id_type=MESH
                    )

    near = []
    for way, (side, sends, gets) in enumerate((up, down)):
        copy = pltpu.make_async_remote_copy(
            src_ref=entering.at[0],
            dst_ref=entering.at[1 + way],
            send_sem=near_send.at[way],
            recv_sem=near_recv.at[way],
            device_id=(row, side),
            device_id_type=MESH,
        )
        now = sends if way == 0 else jnp.logical_and(sends, jnp.logical_not(by_slow))
        pl.when(now)(copy.start)
        near.append((copy, sends, gets))

    def goes(place, to, there):
        if to > 0 or place == 1:
            return there
        return jnp.logical_and(there, column > (0 if place == 0 else 1))

    def straight_copy(place, side, to, source):
        return pltpu.make_async_remote_copy(
            src_ref=packed_own,
            dst_ref=straight.at[place, source],
            send_sem=straight_send.at[place, to],
            recv_sem=straight_recv.at[place, source],
            device_id=(to, side),
            device_id_type=MESH,
        )

    @pl.when(late)
    def _():
        for to in range(quarter_rows):
            for place, side, there in columns:
                copy = straight_copy(place, side, to, row - half)
                pl.when(goes(place, to, there))(copy.start)

    for load in loads[3:6]:
        load.wait()
    high, low = halves(product(given, inner[...]))
    length = samples // PIECES
    per = length // BLOCK
    pieces = []
    for piece in range(PIECES):
        rows = []
        for k in range(piece * per, (piece + 1) * per):
            k_high = jnp.where(slot == k, high, jnp.zeros_like(high))
            k_low = jnp.where(slot == k, low, jnp.zeros_like(low))
            rows.append(jnp.concatenate([k_high, k_low, k_high], axis=1))
        size = per * channels
        local = product(parts[piece * size : (piece + 1) * size, :], main[...]) + product(
            jnp.concatenate(rows, axis=0), correct[...]
        )
        for k in range(per):
            at = piece * length + k * BLOCK
            x[:, at : at + BLOCK] = local[k * channels : (k + 1) * channels]
        span = pl.ds(piece * length, length)
        pair = []
        for way, ((side, sends, gets), source, target) in enumerate(
            ((up, channels - RADIUS, 0), (down, 0, RADIUS))
        ):
            copy = pltpu.make_async_remote_copy(
                src_ref=x.at[pl.ds(source, RADIUS), span],
                dst_ref=halo.at[pl.ds(target, RADIUS), span],
                send_sem=halo_send.at[way, piece],
                recv_sem=halo_recv.at[way, piece],
                device_id=(row, side),
                device_id_type=MESH,
            )
            now = sends if way == 0 else jnp.logical_and(sends, jnp.logical_not(by_slow))
            pl.when(now)(copy.start)
            pair.append((copy, sends, gets))
        pieces.append(pair)
    for load in loads[6:]:
        load.wait()

    @pl.when(by_slow)
    def _():
        pl.semaphore_wait(slow_sem, 1)
        near[1][0].start()
        for pair in pieces:
            pair[1][0].start()

    high, low = halves(x[...])
    out[...] = product(own[...], jnp.concatenate([high, high, low], axis=0))

    def receive(piece):
        for copy, sends, gets in pieces[piece]:
            pl.when(gets)(copy.wait_recv)
        begin, end = piece * length, (piece + 1) * length
        high, low = halves(halo[:, begin:end])
        out[:, begin:end] += product(edge[...], jnp.concatenate([high, high, low], axis=0))

    for copy, sends, gets in near:
        pl.when(gets)(copy.wait_recv)
    mine = product_turned(
        tripled(jnp.concatenate([entering[0], entering[1], entering[2]], axis=1), 1), states[...]
    )
    ends[row] = jnp.concatenate([mine[2 * k : 2 * k + 2] for k in range(4)], axis=1)

    def end_copy(to, slot_index):
        return pltpu.make_async_remote_copy(
            src_ref=ends.at[slot_index],
            dst_ref=ends.at[slot_index],
            send_sem=end_send.at[to],
            recv_sem=end_recv.at[slot_index],
            device_id=(to, column),
            device_id_type=MESH,
        )

    awaited = [len([to for source, to in answers if to == at]) for at in range(half)]

    @pl.when(jnp.logical_and(is_one_of(chip, [at for at in range(half) if awaited[at]]), quick))
    def _():
        pl.semaphore_wait(answer_sem, pick(awaited))

    def to_send(step):
        to = lax.rem(row + step, devices)
        to_slow = jnp.logical_and(to == 0, column == 0)
        return to, jnp.logical_and(
            jnp.logical_or(early, to >= quarter_rows), jnp.logical_not(to_slow)
        )

    def to_get(step):
        source = lax.rem(row + step, devices)
        return source, jnp.logical_or(jnp.logical_not(direct), source < half)

    for step in order:
        to, there = to_send(step)
        pl.when(there)(end_copy(to, row).start)

    in_column = jnp.logical_and(column == 0, row > 0)

    @pl.when(in_column)
    def _():
        pl.semaphore_wait(slow_sem, 1)
        end_copy(0, row).start()

    for piece in range(EARLY):
        receive(piece)

    for step in order:
        to, there = to_send(step)
        pl.when(there)(end_copy(to, row).wait_send)
    pl.when(in_column)(end_copy(0, row).wait_send)

    @pl.when(late)
    def _():
        for to in range(quarter_rows):
            for place, side, there in columns:
                copy = straight_copy(place, side, to, row - half)
                pl.when(goes(place, to, there))(copy.wait_send)

    for copy, sends, gets in near + [copy for pair in pieces[:-1] for copy in pair]:
        pl.when(sends)(copy.wait_send)

    for step in reversed(order):
        source, there = to_get(step)
        pl.when(there)(end_copy(row, source).wait_recv)

    def unpacked(value):
        folded = [
            pltpu.roll(value[8 * k : 8 * k + 8], LANES - 32 * k, axis=1) for k in range(1, 4)
        ]
        return value[0:8] + functools.reduce(jnp.add, folded)

    @pl.when(direct)
    def _():
        for source in range(half):
            for place, side, there in ((0, column, True), (1, below, up[2]), (2, above, down[2])):
                copy = straight_copy(place, side, 0, source)
                if place == 0:
                    copy.wait_recv()
                else:
                    pl.when(there)(copy.wait_recv)
        lane = lax.broadcasted_iota(jnp.int32, (8, LANES), 1)
        gathered = []
        for place in range(3):
            value = jnp.concatenate([straight[place, k] for k in range(half)], axis=0)
            value = unpacked(product(later[...], tripled(value, 0)))
            gathered.append(jnp.where(lane < channels, value, 0.0))
        extra[:, :channels] = product_turned(
            tripled(jnp.concatenate(gathered, axis=1), 1), states[...]
        )

    packed = jnp.concatenate([ends[k] for k in range(devices)], axis=0)
    mixed = product(across[...], tripled(packed, 0))
    taken = (unpacked(mixed) + extra[...])[:, :channels]

    for piece in range(EARLY, PIECES):
        receive(piece)

    out[...] += lax.dot_general(
        tripled(taken, 0),
        outside[...],
        (((0,), (0,)), ((), ())),
        preferred_element_type=jnp.float32,
    )

    for copy, sends, gets in pieces[-1]:
        pl.when(sends)(copy.wait_send)


def shards(devices, groups, strain, channel_mask):
    channels, samples = strain.shape
    tables = filter_tables(samples // BLOCK, devices) + space_tables(channels)
    tables = [jnp.asarray(table) for table in tables]
    f32 = jnp.float32
    held = [pltpu.VMEM(table.shape, table.dtype) for table in tables]
    for k in (5, 6):
        held[k] = pltpu.VMEM(tables[k].shape[1:], tables[k].dtype)
    return pl.pallas_call(
        functools.partial(kernel, devices, groups),
        out_shape=jax.ShapeDtypeStruct((channels, samples), f32),
        in_specs=[pl.BlockSpec(memory_space=pltpu.HBM)] * (2 + len(tables)),
        out_specs=pl.BlockSpec(memory_space=pltpu.VMEM),
        scratch_shapes=[
            pltpu.VMEM((channels, samples), f32),
            pltpu.VMEM((1, channels), jnp.int32),
            *held,
            pltpu.VMEM((2 * RADIUS, samples), f32),
            pltpu.VMEM((devices, 2, LANES), f32),
            pltpu.VMEM((3, 8, LANES), f32),
            pltpu.VMEM((3, devices // 2, 2, LANES), f32),
            pltpu.VMEM((2, LANES), f32),
            pltpu.VMEM((8, LANES), f32),
            pltpu.VMEM((channels * samples // BLOCK, 3 * BLOCK), jnp.bfloat16),
            pltpu.SemaphoreType.DMA((2 + len(tables),)),
            pltpu.SemaphoreType.DMA((LOADS,)),
            pltpu.SemaphoreType.DMA((devices,)),
            pltpu.SemaphoreType.DMA((devices,)),
            pltpu.SemaphoreType.DMA((2,)),
            pltpu.SemaphoreType.DMA((2,)),
            pltpu.SemaphoreType.DMA((2, PIECES)),
            pltpu.SemaphoreType.DMA((2, PIECES)),
            pltpu.SemaphoreType.DMA((3, devices // 2)),
            pltpu.SemaphoreType.DMA((3, devices // 2)),
            pltpu.SemaphoreType.REGULAR,
            pltpu.SemaphoreType.REGULAR,
        ],
        compiler_params=pltpu.CompilerParams(
            collective_id=0, has_side_effects=True, vmem_limit_bytes=40 * 1024 * 1024
        ),
        name="bandpass",
    )(
        *[
            pltpu.with_memory_space_constraint(value, pltpu.HBM)
            for value in (strain, channel_mask.reshape(1, channels), *tables)
        ]
    )


def solution(mesh):
    placed = (P("chan", "tm"), P("chan"))
    sizes = dict(zip(mesh.axis_names, mesh.devices.shape))
    return jax.shard_map(
        functools.partial(shards, sizes["tm"], sizes["chan"]),
        mesh=mesh,
        in_specs=placed,
        out_specs=P("chan", "tm"),
        check_vma=False,
    )
```
